32 devices in a mesh: groups: 2 (over y), rows: 4 (over z), cols: 2 (over x), date: 2 (over core).
Axes of the slice: x: 2, y: 2, z: 4, core: 2. Of those that a mesh axis runs over, the one named last changes fastest.
Arguments:
- features: bfloat16 [2, 128, 256, 128], P('date', ('groups', 'rows'), 'cols'), parts along dimension 1, may hold values from -6 to 6
- scene_shift: int32 [8, 2, 2], P('groups'), parts along dimension 0, may hold values from -4 to 4, as said below
- w_lat: bfloat16 [128, 128], replicated, may hold values from -0.5 to 0.5
- b_lat: float32 [128], replicated, may hold values from -3 to 3
- w_fpn: bfloat16 [3, 3, 128, 128], replicated, may hold values from -0.1875 to 0.1875
- w_dec1: bfloat16 [3, 3, 128, 128], replicated, may hold values from -0.1875 to 0.1875
- b_dec1: float32 [128], replicated, may hold values from -3 to 3
- w_dec2: bfloat16 [3, 3, 128, 128], replicated, may hold values from -0.1875 to 0.1875
- b_dec2: float32 [128], replicated, may hold values from -3 to 3
- w_out: bfloat16 [128], replicated, may hold values from -0.5 to 0.5
- b_out: float32 [1], replicated, may hold values from -3 to 3
Outputs:
- change_logit: float32 [128, 256], P(('groups', 'rows', 'date'), 'cols'), parts along dimension 0
The draws below stay inside these ranges and needn't reach their ends.
There are 2 independent parts, one for each index of `groups`. The reference program is written for one: setup_inputs(seed, part) draws one part's arguments, and reference() takes and returns one part's arrays. A program takes and returns all parts, laid end to end along the dimension named above; an argument that names none is the same for every part. Nothing has to cross between parts.
Inputs may be any that keep to these rules, and one draw needn't show every extreme that they name: `scene_shift`: each offset component lies between -4 and 4; 4 and -4 both occur in every draw.
All inputs are finite; a program needn't handle non-finite values.
Results may differ from the reference program's by a relative error of at most 0.0076.
Values may be sent and summed in bfloat16 or wider, within the bound.
No kernel may reach another device: no remote copies, remote signals or barrier semaphores. Data moves between devices by JAX's collectives and lax.ppermute only.
A program may use at most 64 MiB of HBM per device.

```python
import jax
import jax.numpy as jnp
from jax import lax

C = 128
CIN = 128
TH = 16
TW = 128
MO = 4
TILE_ROWS = 4
TILE_COLS = 2
GH = 64
GW = 256


def draw_scene_shift(key, part):
    base = jax.random.randint(key, (TILE_ROWS, TILE_COLS, 2), -MO, MO + 1).astype(jnp.int32)
    pick_row = jax.random.randint(jax.random.fold_in(key, 7), (), 0, TILE_ROWS)
    pick_col = jax.random.randint(jax.random.fold_in(key, 8), (), 0, TILE_COLS)
    base = base.at[pick_row, pick_col].set(jnp.array([MO, -MO], jnp.int32))
    other_row = (pick_row + TILE_ROWS // 2) % TILE_ROWS
    base = base.at[other_row, pick_col].set(jnp.array([-MO, MO], jnp.int32))
    return base


def levels(own_key, extent, pieces, low, top_value):
    level, own = 1.0, jax.random.fold_in(own_key, 6)
    for axis_at, blocks in pieces:
        steps = jnp.exp(jax.random.uniform(jax.random.fold_in(own, axis_at), (blocks,), jnp.float32, low / len(pieces), top_value / len(pieces)))
        level = level * jnp.repeat(steps, extent[axis_at] // blocks).reshape([-1 if axis == axis_at else 1 for axis in range(len(extent))])
    return level


def scatter_about(own_key, dims, deviation, most, shards=(), held_as=jnp.bfloat16):
    drawn = deviation * jax.random.normal(own_key, dims, jnp.float32)
    if shards:
        drawn = drawn * levels(own_key, dims, shards, -0.22, 0.18)
    return jnp.clip(drawn, -most, most).astype(held_as)


def setup_inputs(seed: int = 0, part: int = 0) -> dict:
    keys = jax.random.split(jax.random.key(seed), 12)
    part_keys = jax.random.split(jax.random.fold_in(keys[11], part), 12)
    return {
        "features": scatter_about(part_keys[0], (2, GH, GW, CIN), 1.0, 6.0, ((0, 2), (1, 4), (2, 2))),
        "scene_shift": draw_scene_shift(jax.random.fold_in(jax.random.fold_in(keys[11], part), 71), part),
        "w_lat": scatter_about(keys[2], (CIN, C), CIN ** -0.5, 0.5),
        "b_lat": scatter_about(keys[3], (C,), 0.5, 3.0, (), jnp.float32),
        "w_fpn": scatter_about(keys[4], (3, 3, C, C), (9 * C) ** -0.5, 0.1875),
        "w_dec1": scatter_about(keys[5], (3, 3, C, C), (9 * C) ** -0.5, 0.1875),
        "b_dec1": scatter_about(keys[6], (C,), 0.5, 3.0, (), jnp.float32),
        "w_dec2": scatter_about(keys[7], (3, 3, C, C), (9 * C) ** -0.5, 0.1875),
        "b_dec2": scatter_about(keys[8], (C,), 0.5, 3.0, (), jnp.float32),
        "w_out": scatter_about(keys[9], (C,), C ** -0.5, 0.5),
        "b_out": scatter_about(keys[10], (1,), 1.0, 3.0, (), jnp.float32),
    }


def conv_three(padded, weights):
    out_rows = padded.shape[0] - 2
    out_cols = padded.shape[1] - 2
    channels = padded.shape[2]
    total = jnp.zeros((out_rows * out_cols, weights.shape[3]), jnp.float32)
    for row_tap in range(3):
        for col_tap in range(3):
            window = padded[row_tap:row_tap + out_rows, col_tap:col_tap + out_cols].reshape(-1, channels)
            total = total + jnp.dot(window, weights[row_tap, col_tap], preferred_element_type=jnp.float32)
    return total.reshape(out_rows, out_cols, weights.shape[3])


def pad_one(field):
    return jnp.pad(field, ((1, 1), (1, 1), (0, 0)))


def reference(features, scene_shift, w_lat, b_lat, w_fpn, w_dec1, b_dec1, w_dec2, b_dec2, w_out, b_out):
    rows_all = features.shape[1]
    cols_all = features.shape[2]
    lateral = (jnp.dot(features.reshape(-1, CIN), w_lat, preferred_element_type=jnp.float32) + b_lat).astype(jnp.bfloat16)
    lateral = lateral.reshape(2, rows_all, cols_all, C)
    pyramid_a = conv_three(pad_one(lateral[0]), w_fpn).astype(jnp.bfloat16)
    pyramid_b = conv_three(pad_one(lateral[1]), w_fpn).astype(jnp.bfloat16)
    canvas = jnp.zeros((rows_all + 2 * MO, cols_all + 2 * MO, C), jnp.float32)
    counts = jnp.zeros((rows_all + 2 * MO, cols_all + 2 * MO), jnp.float32)

    def place(index, carry):
        canvas, counts = carry
        index = jnp.asarray(index).astype(jnp.int32)
        scene_row = index // TILE_COLS
        scene_col = index % TILE_COLS
        top = (scene_row * TH + scene_shift[scene_row, scene_col, 0] + MO).astype(jnp.int32)
        left = (scene_col * TW + scene_shift[scene_row, scene_col, 1] + MO).astype(jnp.int32)
        zero = jnp.zeros((), jnp.int32)
        piece = lax.dynamic_slice(pyramid_b, ((scene_row * TH).astype(jnp.int32), (scene_col * TW).astype(jnp.int32), zero), (TH, TW, C)).astype(jnp.float32)
        region = lax.dynamic_slice(canvas, (top, left, zero), (TH, TW, C))
        canvas = lax.dynamic_update_slice(canvas, region + piece, (top, left, zero))
        region_count = lax.dynamic_slice(counts, (top, left), (TH, TW))
        counts = lax.dynamic_update_slice(counts, region_count + jnp.float32(1.0), (top, left))
        return canvas, counts

    canvas, counts = lax.fori_loop(0, TILE_ROWS * TILE_COLS, place, (canvas, counts))
    b_sum = canvas[MO:MO + rows_all, MO:MO + cols_all]
    coverage = counts[MO:MO + rows_all, MO:MO + cols_all]
    regridded = b_sum / jnp.maximum(coverage, 1.0)[:, :, None]
    covered = jnp.minimum(coverage, 1.0)[:, :, None]
    difference = (jnp.abs(pyramid_a.astype(jnp.float32) - regridded) * covered).astype(jnp.bfloat16)
    hidden_one = jnp.maximum(conv_three(pad_one(difference), w_dec1) + b_dec1, 0.0).astype(jnp.bfloat16)
    hidden_two = jnp.maximum(conv_three(pad_one(hidden_one), w_dec2) + b_dec2, 0.0).astype(jnp.bfloat16)
    logit = jnp.dot(hidden_two.reshape(-1, C), w_out, preferred_element_type=jnp.float32) + b_out
    return logit.reshape(rows_all, cols_all)
```

```python
import functools

import jax
import jax.numpy as jnp
from jax import lax
from jax.experimental import pallas as pl
from jax.experimental.pallas import tpu as pltpu
from jax.sharding import PartitionSpec as P

MO = 4
HA = 3
HB = HA + MO
CW = 8
F32 = jnp.float32
BF16 = jnp.bfloat16


def column_partner(col, parity, n_cols):
    right = col % 2 == parity
    return (col + 1) % n_cols if right else (col - 1) % n_cols


def row_partner(row, date, n_rows):
    near = row + (1 if date else -1)
    return (near, 1 - date) if 0 <= near < n_rows else None


def send(value, sizes, target):
    n_rows, n_cols, n_dates = sizes
    pairs = []
    for row in range(n_rows):
        for col in range(n_cols):
            for date in range(n_dates):
                to_row, to_col, to_date = target(row, col, date)
                source = (row * n_cols + col) * n_dates + date
                pairs.append((source, (to_row * n_cols + to_col) * n_dates + to_date))
    return lax.ppermute(value, ("rows", "cols", "date"), pairs)


def conv_weights(w_ref):
    chans = w_ref.shape[-1]
    tall = w_ref[...].reshape(-1, chans)
    none = jnp.zeros((3 * chans, chans), tall.dtype)
    return jnp.concatenate(
        [jnp.concatenate([tall, none], axis=0), jnp.concatenate([none, tall], axis=0)], axis=1
    )


def body(
    n_par, n_rows, n_cols, tile_rows, tile_cols,
    shift, own, oth, *refs,
):
    sides = refs[:n_par]
    v_ref = refs[n_par]
    corners = refs[n_par + 1 : 2 * n_par + 1]
    (w_lat, b_lat, w_fpn, w_dec1, b_dec1, w_dec2, b_dec2, w_out, b_out, out_ref,
     lat, cat_a, cat_b, pyr_a, pyr_b, dif, cat_d, hid, cat_h) = refs[2 * n_par + 1 :]
    row, col, date = lax.axis_index("rows"), lax.axis_index("cols"), lax.axis_index("date")
    half = tile_rows // 2
    width = tile_cols + 2 * CW
    chans = own.shape[-1]
    first_half = row * 2 + date
    other = 1 - date
    has_row = jnp.where(date == 0, row > 0, row < n_rows - 1)
    row_keep = has_row.astype(F32)

    def at(line, column):
        return CW + line * width + CW + column

    weight, bias = w_lat[...], b_lat[...]

    def lateral(x):
        return jnp.dot(x.reshape(-1, chans), weight, preferred_element_type=F32) + bias

    if n_cols == 2:
        blank = jnp.zeros((CW, chans), F32)
        at_blank = jnp.where(col % 2 == 0, -CW, tile_cols)
        for which in range(2):
            for line in range(tile_rows + 2 * HB):
                lat[which, pl.ds(pl.multiple_of(at(line, at_blank), 8), CW)] = blank
    for which, x_ref in ((date, own), (other, oth)):
        z = lateral(x_ref[...])
        for t in range(tile_rows):
            lat[which, at(t + HB, 0) : at(t + HB, 0) + tile_cols] = z[
                t * tile_cols : (t + 1) * tile_cols
            ]
    base_a = jnp.where(date == 0, HB - HA, HB + tile_rows)
    base_b = jnp.where(date == 0, 0, HB + tile_rows)
    z = lateral(v_ref[...]) * row_keep
    for i in range(HA + HB):
        which, line = (0, base_a + i) if i < HA else (1, base_b + i - HA)
        lat[which, pl.ds(pl.multiple_of(at(line, 0), 8), tile_cols)] = z[
            i * tile_cols : (i + 1) * tile_cols
        ]
    for parity in range(n_par):
        right = col % 2 == parity
        exists = jnp.where(right, col < n_cols - 1, col > 0).astype(F32)
        at_col = jnp.where(right, tile_cols, -CW)
        z = lateral(sides[parity][...]) * exists
        for t in range(2 * tile_rows):
            which = date if t < tile_rows else other
            line = t % tile_rows + HB
            lat[which, pl.ds(pl.multiple_of(at(line, at_col), 8), CW)] = z[t * CW : (t + 1) * CW]
        z = lateral(corners[parity][...]) * (exists * row_keep)
        for i in range(HA + HB):
            which, line = (0, base_a + i) if i < HA else (1, base_b + i - HA)
            lat[which, pl.ds(pl.multiple_of(at(line, at_col), 8), CW)] = z[i * CW : (i + 1) * CW]

    def gather(source, line0, cat, lines, count, column):
        def step(i, carry):
            start = (line0 + i) * width + CW + CW + column
            for tap in range(3):
                cat[i, :, tap * chans : (tap + 1) * chans] = source[
                    pl.ds(start + (tap - 1), count)
                ].astype(BF16)
            return carry

        lax.fori_loop(0, lines, step, 0)

    def conv(cat, pairs, big):
        lines = [
            jnp.concatenate([cat[2 * i + j] for i in range(pairs)], axis=0) for j in range(4)
        ]
        return jnp.dot(jnp.concatenate(lines, axis=1), big, preferred_element_type=F32)

    big = conv_weights(w_fpn)
    lines_a, lines_b = half + 4, half + 4 + 2 * MO
    gather(lat.at[0], HB - HA + half * date, cat_a, lines_a + 2, width, -CW)
    gather(lat.at[1], half * date, cat_b, lines_b + 2, width, -CW)
    z = conv(cat_a, lines_a // 2, big).astype(BF16)
    for i in range(lines_a // 2):
        for k in range(2):
            pyr_a[2 * i + k] = z[i * width : (i + 1) * width, k * chans : (k + 1) * chans]
    z = conv(cat_b, lines_b // 2, big).astype(BF16).astype(F32)
    for i in range(lines_b // 2):
        for k in range(2):
            start = CW + (2 * i + k) * width
            pyr_b[start : start + width] = z[
                i * width : (i + 1) * width, k * chans : (k + 1) * chans
            ]

    near_row = jnp.clip(row + jnp.where(date == 0, -1, 1), 0, n_rows - 1)
    cells = lax.broadcasted_iota(jnp.int32, (width, chans), 0) - CW
    in_cols = ((cells + col * tile_cols >= 0) & (cells + col * tile_cols < n_cols * tile_cols)).astype(F32)
    tiles = []
    for is_near in (False, True):
        for step in (0, -1, 1):
            r = near_row if is_near else row
            c = jnp.clip(col + step, 0, n_cols - 1)
            there = (col + step >= 0) & (col + step < n_cols)
            if is_near:
                there = there & has_row
            sy, sx = shift[r, c, 0], shift[r, c, 1]
            low = sx + step * tile_cols
            lo, n = {0: (0, width), -1: (0, 16), 1: (width - 16, 16)}[step]
            x = cells[lo : lo + n]
            cols = ((x >= low) & (x < low + tile_cols)).astype(F32) * there.astype(F32)
            tiles.append((is_near, lo, n, sy, sx, cols))

    def line_step(y, carry):
        total = jnp.zeros((width, chans), F32)
        count = jnp.zeros((width, chans), F32)
        for is_near, lo, n, sy, sx, cols in tiles:
            q = y - 2 - sy
            is_own = jnp.where(date == 0, q >= 0, q < half)
            hit = (~is_own if is_near else is_own).astype(F32)
            mask = cols * hit
            start = CW + (q + 2 + MO) * width + lo - sx
            part = jnp.where(mask > 0, pyr_b[pl.ds(start, n)], 0.0)
            if n < width:
                pad = jnp.zeros((width - n, chans), F32)
                order = (lambda p: [p, pad]) if lo == 0 else (lambda p: [pad, p])
                part, mask = jnp.concatenate(order(part), 0), jnp.concatenate(order(mask), 0)
            total, count = total + part, count + mask
        line = first_half * half + y - 2
        in_row = ((line >= 0) & (line < n_rows * tile_rows)).astype(F32)
        level = total / jnp.maximum(count, 1.0)
        value = jnp.abs(pyr_a[y].astype(F32) - level)
        value = jnp.where(jnp.minimum(count, 1.0) * in_cols * in_row > 0, value, 0.0)
        dif[pl.ds(pl.multiple_of(CW + y * width, 8), width)] = value
        return carry

    lax.fori_loop(0, lines_a, line_step, 0)

    gather(dif, 0, cat_d, half + 4, width, -CW)
    z = jnp.maximum(conv(cat_d, half // 2 + 1, conv_weights(w_dec1)) + jnp.concatenate([b_dec1[...]] * 2, 1), 0.0)
    for i in range(half // 2 + 1):
        for k in range(2):
            y = 2 * i + k
            line = first_half * half + y - 1
            in_row = ((line >= 0) & (line < n_rows * tile_rows)).astype(F32)
            start = CW + y * width
            hid[start : start + width] = z[
                i * width : (i + 1) * width, k * chans : (k + 1) * chans
            ] * (in_cols * in_row)
    gather(hid, 0, cat_h, half + 2, tile_cols, 0)
    z = jnp.maximum(conv(cat_h, half // 2, conv_weights(w_dec2)) + jnp.concatenate([b_dec2[...]] * 2, 1), 0.0)
    z = z.astype(BF16)
    weight = jnp.broadcast_to(w_out[...], (16, chans))
    for i in range(half // 2):
        for k in range(2):
            logit = lax.dot_general(
                weight,
                z[i * tile_cols : (i + 1) * tile_cols, k * chans : (k + 1) * chans],
                (((1,), (1,)), ((), ())),
                preferred_element_type=F32,
            )
            y = 2 * i + k
            out_ref[y : y + 1] = logit[:1] + b_out[0]


def per_device(
    sizes, features, scene_shift, w_lat, b_lat, w_fpn, w_dec1, b_dec1, w_dec2, b_dec2, w_out, b_out
):
    n_rows, n_cols, _ = sizes
    tile_rows, tile_cols, chans = features.shape[1:]
    col, date = lax.axis_index("cols"), lax.axis_index("date")
    half, width = tile_rows // 2, tile_cols + 2 * CW
    n_par = 1 if n_cols == 2 else 2
    own = features[0]
    oth = send(own, sizes, lambda r, c, d: (r, c, 1 - d))

    def edge(x, parity):
        return jnp.where(col % 2 == parity, x[:, tile_cols - CW :], x[:, :CW])

    first = date == 0
    for_row = jnp.concatenate(
        [
            jnp.where(first, own[:HA], oth[tile_rows - HA :]),
            jnp.where(first, oth[:HB], own[tile_rows - HB :]),
        ],
        axis=0,
    )

    def over(r, c, d, to_col):
        near = row_partner(r, d, n_rows)
        return (r, c ^ 1 if to_col is None else to_col, d) if near is None else (
            near[0], c if to_col is None else to_col, near[1])

    from_row = send(for_row, sizes, lambda r, c, d: over(r, c, d, None))
    sides, corners = [], []
    for parity in range(n_par):
        for_side = jnp.concatenate([edge(own, parity), edge(oth, parity)], axis=0)
        partner = functools.partial(column_partner, parity=parity, n_cols=n_cols)
        sides.append(send(for_side, sizes, lambda r, c, d: (r, partner(c), d)))
        corners.append(
            send(edge(for_row, parity), sizes, lambda r, c, d: over(r, c, d, partner(c)))
        )
    vmem = pl.BlockSpec(memory_space=pltpu.VMEM)
    smem = pl.BlockSpec(memory_space=pltpu.SMEM)
    lines_a, lines_b = half + 4, half + 4 + 2 * MO
    flat = lambda lines: (2 * CW + lines * width, chans)
    return pl.pallas_call(
        functools.partial(body, n_par, n_rows, n_cols, tile_rows, tile_cols),
        out_shape=jax.ShapeDtypeStruct((half, tile_cols), F32),
        in_specs=[smem] + [vmem] * (2 + 2 * n_par + 1) + [vmem] * 8 + [smem],
        out_specs=vmem,
        scratch_shapes=[
            pltpu.VMEM((2,) + flat(tile_rows + 2 * HB), F32),
            pltpu.VMEM((lines_a + 2, width, 3 * chans), BF16),
            pltpu.VMEM((lines_b + 2, width, 3 * chans), BF16),
            pltpu.VMEM((lines_a, width, chans), BF16),
            pltpu.VMEM(flat(lines_b), F32),
            pltpu.VMEM(flat(lines_a), F32),
            pltpu.VMEM((half + 4, width, 3 * chans), BF16),
            pltpu.VMEM(flat(half + 2), F32),
            pltpu.VMEM((half + 2, tile_cols, 3 * chans), BF16),
        ],
        compiler_params=pltpu.CompilerParams(vmem_limit_bytes=40 * 2**20),
        name="change",
    )(
        scene_shift, own, oth, *sides, from_row, *corners,
        w_lat, b_lat[None], w_fpn, w_dec1, b_dec1[None], w_dec2, b_dec2[None], w_out[None], b_out,
    )


def solution(mesh):
    sizes = (mesh.shape["rows"], mesh.shape["cols"], mesh.shape["date"])
    return jax.shard_map(
        functools.partial(per_device, sizes),
        mesh=mesh,
        in_specs=(P("date", ("groups", "rows"), "cols", None), P("groups", None, None)) + (P(),) * 9,
        out_specs=P(("groups", "rows", "date"), "cols"),
        check_vma=False,
    )
```

```python
import functools

import jax
import jax.numpy as jnp
from jax import lax
from jax.experimental import pallas as pl
from jax.experimental.pallas import tpu as pltpu
from jax.sharding import PartitionSpec as P


MO = 4
HA = 3
HB = HA + MO
CW = 8
STRIP = 16
F32 = jnp.float32
BF16 = jnp.bfloat16


def column_partner(col, parity, n_cols):
    right = col % 2 == parity
    return (col + 1) % n_cols if right else (col - 1) % n_cols


def send(value, sizes, target):
    n_groups, n_rows, n_cols, n_dates = sizes

    def place(group, row, col, date):
        return ((group * n_rows + row) * n_cols + col) * n_dates + date

    pairs = []
    for group in range(n_groups):
        for row in range(n_rows):
            for col in range(n_cols):
                for date in range(n_dates):
                    to = target(row, col, date)
                    end = (
                        place((group + 1) % n_groups, row, col, date)
                        if to is None
                        else place(group, *to)
                    )
                    pairs.append((place(group, row, col, date), end))
    return lax.ppermute(value, ("groups", "rows", "cols", "date"), pairs)


def conv_weights(w_ref):
    chans = w_ref.shape[-1]
    tall = w_ref[...].reshape(-1, chans)
    none = jnp.zeros((3 * chans, chans), tall.dtype)
    return jnp.concatenate(
        [jnp.concatenate([tall, none], axis=0), jnp.concatenate([none, tall], axis=0)], axis=1
    )


def at(line, column, width):
    return CW + line * width + CW + column


def position():
    return lax.axis_index("rows"), lax.axis_index("cols"), lax.axis_index("date")


def put(target, line, column, width, value):
    start = at(line, column, width)
    if not isinstance(start, int):
        start = pl.multiple_of(start, 8)
    target[pl.ds(start, value.shape[0])] = value


def gather(source, line, cat, index, count, column, width):
    chans = source.shape[-1]
    start = at(line, column, width)
    for tap in range(3):
        cat[index, :, tap * chans : (tap + 1) * chans] = source[
            pl.ds(start + (tap - 1), count)
        ].astype(BF16)


def conv(parts, big):
    lines = [
        jnp.concatenate(
            [cat[first + 2 * i + j] for cat, first, pairs in parts for i in range(pairs)], axis=0
        )
        for j in range(4)
    ]
    return jnp.dot(jnp.concatenate(lines, axis=1), big, preferred_element_type=F32)


def line_of(z, index, columns):
    chans = z.shape[1] // 2
    pair, k = divmod(index, 2)
    return z[pair * columns : (pair + 1) * columns, k * chans : (k + 1) * chans]


def tile_columns(row, col, there, shift, n_cols, tile_cols, width, chans):
    cells = lax.broadcasted_iota(jnp.int32, (width, chans), 0) - CW
    tiles = []
    for step in (0, -1, 1):
        c = jnp.clip(col + step, 0, n_cols - 1)
        is_tile = there & (col + step >= 0) & (col + step < n_cols)
        sy, sx = shift[row, c, 0], shift[row, c, 1]
        low = sx + step * tile_cols
        lo, n = {0: (0, width), -1: (0, STRIP), 1: (width - STRIP, STRIP)}[step]
        x = cells[lo : lo + n]
        mask = ((x >= low) & (x < low + tile_cols)).astype(F32) * is_tile.astype(F32)
        tiles.append((sy, sx, lo, mask))
    return tiles


def spread(full, left, right):
    return jnp.concatenate(
        [full[:STRIP] + left, full[STRIP:-STRIP], full[-STRIP:] + right], axis=0
    )


def placed(pyr_b, q_of, tiles, hits, width):
    parts = []
    for (sy, sx, lo, mask), hit in zip(tiles, hits, strict=True):
        start = CW + (q_of(sy) + 2 + MO) * width + lo - sx
        value = pyr_b[pl.ds(start, mask.shape[0])] * mask
        parts.append(value if hit is None else value * hit)
    return spread(*parts)


def grid_columns(col, n_cols, tile_cols, width, chans):
    x = lax.broadcasted_iota(jnp.int32, (width, chans), 0) - CW + col * tile_cols
    return ((x >= 0) & (x < n_cols * tile_cols)).astype(F32)


def in_grid(line, n_rows, tile_rows):
    return ((line >= 0) & (line < n_rows * tile_rows)).astype(F32)


def blank_side(lat, lines, col, tile_cols, width):
    column = jnp.where(col % 2 == 0, -CW, tile_cols)
    for line in range(lines):
        put(lat, line, column, width, jnp.zeros((CW, lat.shape[-1]), F32))


def side_of(parity, col, n_cols, tile_cols):
    right = col % 2 == parity
    exists = jnp.where(right, col < n_cols - 1, col > 0).astype(F32)
    return jnp.where(right, tile_cols, -CW), exists


def inner_body(n_par, n_rows, n_cols, tile_rows, tile_cols, shift, own, oth, *refs):
    mine, others = refs[:n_par], refs[n_par : 2 * n_par]
    (w_lat, b_lat, w_fpn, w_dec1, b_dec1,
     pyr_a, pyr_b, cat_a, cat_b, cat_d, hid, lat, dif) = refs[2 * n_par :]
    row, col, date = position()
    half, width, chans = tile_rows // 2, tile_cols + 2 * CW, own.shape[-1]
    weight, bias = w_lat[...], b_lat[...]
    first_half = row * 2 + date

    def lateral(x):
        return jnp.dot(x.reshape(-1, chans), weight, preferred_element_type=F32) + bias

    for which, x_ref, side_refs in ((date, own, mine), (1 - date, oth, others)):
        flat = lat.at[which]
        z = lateral(x_ref[...])
        for t in range(tile_rows):
            put(flat, t, 0, width, z[t * tile_cols : (t + 1) * tile_cols])
        if n_cols == 2:
            blank_side(flat, tile_rows, col, tile_cols, width)
        for parity in range(n_par):
            column, exists = side_of(parity, col, n_cols, tile_cols)
            z = lateral(side_refs[parity][...]) * exists
            for t in range(tile_rows):
                put(flat, t, column, width, z[t * CW : (t + 1) * CW])

    for j in range(half + HA):
        gather(lat.at[0], j + (half - HA) * date, cat_a, j + date, width, -CW, width)
    for j in range(half + HB):
        gather(lat.at[1], j + (half - HB) * date, cat_b, j + date, width, -CW, width)
    pairs_a, pairs_b = half // 2, half // 2 + MO // 2
    z = conv([(cat_a, 1, pairs_a), (cat_b, 1, pairs_b)], conv_weights(w_fpn)).astype(BF16)
    for i in range(2 * pairs_a):
        pyr_a[i + 4 * (1 - date)] = line_of(z, i, width)
    pyr_b[:CW] = jnp.zeros((CW, chans), F32)
    pyr_b[pyr_b.shape[0] - CW :] = jnp.zeros((CW, chans), F32)
    for i in range(2 * pairs_b):
        put(pyr_b, i + (4 + MO) * (1 - date), -CW, width, line_of(z, 2 * pairs_a + i, width).astype(F32))

    tiles = tile_columns(row, col, row >= 0, shift, n_cols, tile_cols, width, chans)
    count = spread(*[mask for *_, mask in tiles])
    inside = grid_columns(col, n_cols, tile_cols, width, chans)
    share = 1.0 / jnp.maximum(count, 1.0)
    keep = jnp.minimum(count, 1.0) * inside
    for i in range(4):
        y = i + half * (1 - date)
        level = placed(pyr_b, lambda sy, y=y: y - 2 - sy, tiles, [None] * 3, width) * share
        value = jnp.abs(pyr_a[y].astype(F32) - level)
        line = first_half * half + y - 2
        put(dif, i, -CW, width, value * (keep * in_grid(line, n_rows, tile_rows)))
    for i in range(4):
        gather(dif, i, cat_d, i, width, -CW, width)
    z = conv([(cat_d, 0, 1)], conv_weights(w_dec1))
    z = jnp.maximum(z + jnp.concatenate([b_dec1[...]] * 2, 1), 0.0)
    for i in range(2):
        line = first_half * half + i + half * (1 - date) - 1
        put(hid, i, -CW, width, line_of(z, i, width) * (inside * in_grid(line, n_rows, tile_rows)))


def outer_body(n_par, n_rows, n_cols, tile_rows, tile_cols, shift, v_ref, *refs):
    corners = refs[:n_par]
    (_, _, t_a, t_b, t_d, t_h, w_lat, b_lat, w_fpn, w_dec1, b_dec1, w_dec2, b_dec2, w_out, b_out,
     out_ref, pyr_a, pyr_b, lat, cat_a, cat_b, dif, cat_d, hid, cat_h) = refs[n_par:]
    row, col, date = position()
    half, width, chans = tile_rows // 2, tile_cols + 2 * CW, w_lat.shape[-1]
    first_half = row * 2 + date
    has_row = jnp.where(date == 0, row > 0, row < n_rows - 1)
    row_keep = has_row.astype(F32)
    weight, bias = w_lat[...], b_lat[...]

    def lateral(x):
        return jnp.dot(x.reshape(-1, chans), weight, preferred_element_type=F32) + bias

    z = lateral(v_ref[...]) * row_keep
    for i in range(HA + HB):
        put(lat, i, 0, width, z[i * tile_cols : (i + 1) * tile_cols])
    if n_cols == 2:
        blank_side(lat, HA + HB, col, tile_cols, width)
    for parity in range(n_par):
        column, exists = side_of(parity, col, n_cols, tile_cols)
        z = lateral(corners[parity][...]) * (exists * row_keep)
        for i in range(HA + HB):
            put(lat, i, column, width, z[i * CW : (i + 1) * CW])
    for i in range(3):
        cat_a[i + HA * (1 - date)] = t_a[i + (half + 1) * date]
        cat_b[i + HB * (1 - date)] = t_b[i + (half + MO + 1) * date]
    for i in range(HA):
        gather(lat, i, cat_a, i + 3 * date, width, -CW, width)
    for i in range(HB):
        gather(lat, i + HA, cat_b, i + 3 * date, width, -CW, width)
    pairs_b = 2 + MO // 2
    z = conv([(cat_a, 0, 2), (cat_b, 0, pairs_b)], conv_weights(w_fpn)).astype(BF16)
    for i in range(4):
        pyr_a[i + half * date] = line_of(z, i, width)
    for i in range(2 * pairs_b):
        put(pyr_b, i + (half + MO) * date, -CW, width, line_of(z, 4 + i, width).astype(F32))

    near_row = jnp.clip(row + jnp.where(date == 0, -1, 1), 0, n_rows - 1)
    tiles = tile_columns(row, col, row >= 0, shift, n_cols, tile_cols, width, chans)
    near = tile_columns(near_row, col, has_row, shift, n_cols, tile_cols, width, chans)
    inside = grid_columns(col, n_cols, tile_cols, width, chans)
    for i in range(half):
        y = i + 4 * date
        q_of = lambda sy, y=y: y - 2 - sy

        def is_own(sy):
            return jnp.where(date == 0, q_of(sy) >= 0, q_of(sy) < half).astype(F32)

        own_hits = [is_own(sy) for sy, *_ in tiles]
        near_hits = [1.0 - is_own(sy) for sy, *_ in near]
        total = placed(pyr_b, q_of, tiles, own_hits, width) + placed(pyr_b, q_of, near, near_hits, width)
        count = spread(*[t[-1] * h for t, h in zip(tiles, own_hits)]) + spread(*[t[-1] * h for t, h in zip(near, near_hits)])
        value = jnp.abs(pyr_a[y].astype(F32) - total / jnp.maximum(count, 1.0))
        line = first_half * half + y - 2
        keep = jnp.minimum(count, 1.0) * inside * in_grid(line, n_rows, tile_rows)
        put(dif, i, -CW, width, value * keep)

    for i in range(2):
        cat_d[i + half * (1 - date)] = t_d[i + 2 * date]
        put(hid, i + half * (1 - date), -CW, width, t_h[pl.ds(CW + i * width, width)])
    for i in range(half):
        gather(dif, i, cat_d, i + 2 * date, width, -CW, width)
    z = conv([(cat_d, 0, half // 2)], conv_weights(w_dec1))
    z = jnp.maximum(z + jnp.concatenate([b_dec1[...]] * 2, 1), 0.0)
    for i in range(half):
        y = i + 2 * date
        line = first_half * half + y - 1
        put(hid, y, -CW, width, line_of(z, i, width) * (inside * in_grid(line, n_rows, tile_rows)))
    for i in range(half + 2):
        gather(hid, i, cat_h, i, tile_cols, 0, width)
    z = conv([(cat_h, 0, half // 2)], conv_weights(w_dec2))
    z = jnp.maximum(z + jnp.concatenate([b_dec2[...]] * 2, 1), 0.0).astype(BF16)
    weight = jnp.broadcast_to(w_out[...], (16, chans))
    for i in range(half):
        logit = lax.dot_general(
            weight, line_of(z, i, tile_cols), (((1,), (1,)), ((), ())), preferred_element_type=F32
        )
        out_ref[i : i + 1] = logit[:1] + b_out[0]


def per_device(
    sizes, features, scene_shift, w_lat, b_lat, w_fpn, w_dec1, b_dec1, w_dec2, b_dec2, w_out, b_out
):
    _, n_rows, n_cols, _ = sizes
    tile_rows, tile_cols, chans = features.shape[1:]
    col, date = lax.axis_index("cols"), lax.axis_index("date")
    half, width = tile_rows // 2, tile_cols + 2 * CW
    n_par = 1 if n_cols == 2 else 2
    own = features[0]
    first = date == 0

    def swap(value):
        return send(value, sizes, lambda r, c, d: (r, c, 1 - d))

    def edge(x, parity):
        return jnp.where(col % 2 == parity, x[:, tile_cols - CW :], x[:, :CW])

    def partner(c, parity):
        return column_partner(c, parity, n_cols)

    oth = swap(own)

    def shift_row(r, c, d):
        near = r - 1 + 2 * d
        return (near, c, 1 - d) if 0 <= near < n_rows else None

    def corner(p, r, c, d):
        near = shift_row(r, c, d)
        return None if near is None else (near[0], partner(c, p), near[2])

    mine, corners, others = [], [], []
    for p in range(n_par):
        mine.append(send(edge(own, p), sizes, lambda r, c, d, p=p: (r, partner(c, p), d)))
    rows_own = lax.dynamic_slice_in_dim(own, (tile_rows - HB) * date, HB, 0)
    rows_own = lax.optimization_barrier(rows_own)
    rows_oth = lax.dynamic_slice_in_dim(oth, (tile_rows - HB) * date, HB, 0)
    for_row = jnp.concatenate(
        [
            jnp.where(first, rows_own[:HA], rows_oth[HB - HA :]),
            jnp.where(first, rows_oth, rows_own),
        ],
        axis=0,
    )
    from_row = send(for_row, sizes, shift_row)
    for p in range(n_par):
        corners.append(send(edge(for_row, p), sizes, functools.partial(corner, p)))
    for p in range(n_par):
        others.append(swap(mine[p]))

    vmem = pl.BlockSpec(memory_space=pltpu.VMEM)
    smem = pl.BlockSpec(memory_space=pltpu.SMEM)
    lines_a, lines_b = half + 4, half + 4 + 2 * MO

    def flat(lines, kind=F32):
        return jax.ShapeDtypeStruct((2 * CW + lines * width, chans), kind)

    def cat(lines, columns=width):
        return jax.ShapeDtypeStruct((lines, columns, 3 * chans), BF16)

    def scratch(shape):
        return pltpu.VMEM(shape.shape, shape.dtype)

    row_a = jax.ShapeDtypeStruct((lines_a, width, chans), BF16)
    lat_tile = flat(tile_rows)
    pyr_a, pyr_b, *kept = pl.pallas_call(
        functools.partial(inner_body, n_par, n_rows, n_cols, tile_rows, tile_cols),
        out_shape=(row_a, flat(lines_b), cat(half + HA + 1), cat(half + HB + 1), cat(4), flat(2)),
        in_specs=[smem] + [vmem] * (2 + 2 * n_par + 5),
        out_specs=(vmem,) * 6,
        scratch_shapes=[pltpu.VMEM((2,) + lat_tile.shape, F32), scratch(flat(4))],
        compiler_params=pltpu.CompilerParams(vmem_limit_bytes=24 * 2**20),
        cost_estimate=pl.CostEstimate(
            flops=2 * 10 * width * 1536 * 256, bytes_accessed=8 * 2**20, transcendentals=0
        ),
        name="inner",
    )(scene_shift, own, oth, *mine, *others, w_lat, b_lat[None], w_fpn, w_dec1, b_dec1[None])
    out, _, _ = pl.pallas_call(
        functools.partial(outer_body, n_par, n_rows, n_cols, tile_rows, tile_cols),
        out_shape=(jax.ShapeDtypeStruct((half, tile_cols), F32), row_a, flat(lines_b)),
        in_specs=[smem] + [vmem] * (n_par + 1 + 14) + [smem],
        out_specs=(vmem,) * 3,
        input_output_aliases={n_par + 2: 1, n_par + 3: 2},
        scratch_shapes=[
            scratch(flat(HA + HB)),
            scratch(cat(HA + 3)),
            scratch(cat(HB + 3)),
            scratch(flat(half)),
            scratch(cat(half + 2)),
            scratch(flat(half + 2)),
            scratch(cat(half + 2, tile_cols)),
        ],
        compiler_params=pltpu.CompilerParams(vmem_limit_bytes=24 * 2**20),
        name="outer",
    )(
        scene_shift, from_row, *corners, pyr_a, pyr_b, *kept,
        w_lat, b_lat[None], w_fpn, w_dec1, b_dec1[None], w_dec2, b_dec2[None], w_out[None], b_out,
    )
    return out


def staged(sizes, *args):
    return per_device(sizes, *args)


def solution(mesh):
    sizes = tuple(mesh.shape[axis] for axis in ("groups", "rows", "cols", "date"))
    return jax.shard_map(
        functools.partial(staged, sizes),
        mesh=mesh,
        in_specs=(P("date", ("groups", "rows"), "cols", None), P("groups", None, None)) + (P(),) * 9,
        out_specs=P(("groups", "rows", "date"), "cols"),
        check_vma=False,
    )
```

```python
import functools

import jax
import jax.numpy as jnp
from jax import lax
from jax.experimental import pallas as pl
from jax.experimental.pallas import tpu as pltpu
from jax.sharding import PartitionSpec as P


MO = 4
HA = 3
HB = HA + MO
CW = 8
STRIP = 16
F32 = jnp.float32
BF16 = jnp.bfloat16


def column_partner(col, parity, n_cols):
    right = col % 2 == parity
    return (col + 1) % n_cols if right else (col - 1) % n_cols


def send(value, sizes, target):
    n_groups, n_rows, n_cols, n_dates = sizes

    def place(group, row, col, date):
        return ((group * n_rows + row) * n_cols + col) * n_dates + date

    pairs = []
    for group in range(n_groups):
        for row in range(n_rows):
            for col in range(n_cols):
                for date in range(n_dates):
                    to = target(row, col, date)
                    end = (
                        place((group + 1) % n_groups, row, col, date)
                        if to is None
                        else place(group, *to)
                    )
                    pairs.append((place(group, row, col, date), end))
    return lax.ppermute(value, ("groups", "rows", "cols", "date"), pairs)


def at(line, column, width):
    return CW + line * width + CW + column


def position():
    return lax.axis_index("rows"), lax.axis_index("cols"), lax.axis_index("date")


def put(target, line, column, width, value):
    start = at(line, column, width)
    if not isinstance(start, int):
        start = pl.multiple_of(start, 8)
    target[pl.ds(start, value.shape[0])] = value


def gather(source, line, cat, index, count, column, width):
    start = at(line, column, width)
    for tap in range(3):
        cat[index, tap] = source[pl.ds(start + (tap - 1), count)].astype(BF16)


def conv(parts, w_ref, ways=2):
    taps = w_ref[...].reshape(-1, w_ref.shape[-1])
    none = jnp.zeros((taps.shape[0] // 3, taps.shape[1]), taps.dtype)
    tall = jnp.concatenate(
        [jnp.concatenate([taps, none], axis=0), jnp.concatenate([none, taps], axis=0)], axis=1
    )
    tops = [(cat, first + 2 * i) for cat, first, pairs in parts for i in range(pairs)]
    outs = []
    for way in range(ways):
        some = tops[way * len(tops) // ways : (way + 1) * len(tops) // ways]
        lines = [
            jnp.concatenate([cat[top + j, tap] for cat, top in some], axis=0)
            for j in range(4)
            for tap in range(3)
        ]
        outs.append(jnp.dot(jnp.concatenate(lines, axis=1), tall, preferred_element_type=F32))
    return jnp.concatenate(outs, axis=0)


def line_of(z, index, columns):
    chans = z.shape[1] // 2
    pair, k = divmod(index, 2)
    return z[pair * columns : (pair + 1) * columns, k * chans : (k + 1) * chans]


def tile_columns(row, col, there, shift, n_cols, tile_cols, chans):
    cells = lax.broadcasted_iota(jnp.int32, (STRIP, chans), 0)
    tiles = []
    for step in (0, -1, 1):
        c = jnp.clip(col + step, 0, n_cols - 1)
        is_tile = (there & (col + step >= 0) & (col + step < n_cols)).astype(F32)
        sy, sx = shift[row, c, 0], shift[row, c, 1]
        low = sx + step * tile_cols
        masks = []
        for left in (True, False):
            x = cells + (-CW if left else tile_cols + CW - STRIP)
            masks.append(((x >= low) & (x < low + tile_cols)).astype(F32) * is_tile)
        tiles.append((sy, sx, is_tile, masks[0], masks[1]))
    return tiles


def difference(a_line, pyr_b, q_of, groups, inside, keep_line, width):
    weight, level, count_l, count_r, level_l, level_r = 0.0, None, None, None, None, None
    plus = lambda x, y: y if x is None else x + y
    for tiles, hit_of in groups:
        for k, (sy, sx, is_tile, left, right) in enumerate(tiles):
            start = CW + (q_of(sy) + 2 + MO) * width - sx
            hit = None if hit_of is None else hit_of(sy)
            if k != 2:
                mask = left if hit is None else left * hit
                count_l = plus(count_l, mask)
                level_l = plus(level_l, pyr_b[pl.ds(start, STRIP)] * mask)
            if k != 1:
                mask = right if hit is None else right * hit
                count_r = plus(count_r, mask)
                level_r = plus(level_r, pyr_b[pl.ds(start + width - STRIP, STRIP)] * mask)
            if k == 0:
                value = pyr_b[pl.ds(start + STRIP, width - 2 * STRIP)]
                if hit is None:
                    level = plus(level, value)
                else:
                    weight = weight + hit * is_tile
                    level = plus(level, value * (hit * is_tile))
    a = a_line.astype(F32)
    outs = []
    for part, count, total, edge in (
        (a[:STRIP], count_l, level_l, inside[0]),
        (a[width - STRIP :], count_r, level_r, inside[1]),
    ):
        value = jnp.abs(part - total / jnp.maximum(count, 1.0))
        outs.append(value * (jnp.minimum(count, 1.0) * edge * keep_line))
    if groups[0][1] is None:
        middle = jnp.abs(a[STRIP : width - STRIP] - level) * keep_line
    else:
        share = jnp.where(weight > 1.5, 0.5, 1.0)
        middle = jnp.abs(a[STRIP : width - STRIP] - level * share) * (jnp.minimum(weight, 1.0) * keep_line)
    return jnp.concatenate([outs[0], middle, outs[1]], axis=0)


def grid_columns(col, n_cols, tile_cols, chans):
    x = lax.broadcasted_iota(jnp.int32, (STRIP, chans), 0) + col * tile_cols
    return [
        ((x + at >= 0) & (x + at < n_cols * tile_cols)).astype(F32) for at in (-CW, tile_cols + CW - STRIP)
    ]


def on_grid(line, inside, keep_line):
    return jnp.concatenate(
        [
            line[:STRIP] * (inside[0] * keep_line),
            line[STRIP:-STRIP] * keep_line,
            line[-STRIP:] * (inside[1] * keep_line),
        ],
        axis=0,
    )


def in_grid(line, n_rows, tile_rows):
    return ((line >= 0) & (line < n_rows * tile_rows)).astype(F32)


def blank_side(lat, lines, col, tile_cols, width):
    column = jnp.where(col % 2 == 0, -CW, tile_cols)
    for line in range(lines):
        put(lat, line, column, width, jnp.zeros((CW, lat.shape[-1]), F32))


def side_of(parity, col, n_cols, tile_cols):
    right = col % 2 == parity
    exists = jnp.where(right, col < n_cols - 1, col > 0).astype(F32)
    return jnp.where(right, tile_cols, -CW), exists


def inner_body(n_par, n_rows, n_cols, tile_rows, tile_cols, shift, own, oth, *refs):
    mine, others = refs[:n_par], refs[n_par : 2 * n_par]
    (w_lat, b_lat, w_fpn, w_dec1, b_dec1,
     pyr_a, pyr_b, cat_a, cat_b, cat_d, hid, lat, dif) = refs[2 * n_par :]
    row, col, date = position()
    half, width, chans = tile_rows // 2, tile_cols + 2 * CW, own.shape[-1]
    weight, bias = w_lat[...], b_lat[...]
    first_half = row * 2 + date

    def lateral(x):
        return jnp.dot(x.reshape(-1, chans), weight, preferred_element_type=F32) + bias

    for which, x_ref, side_refs in ((date, own, mine), (1 - date, oth, others)):
        flat = lat.at[which]
        z = lateral(x_ref[...])
        for t in range(tile_rows):
            put(flat, t, 0, width, z[t * tile_cols : (t + 1) * tile_cols])
        if n_cols == 2:
            blank_side(flat, tile_rows, col, tile_cols, width)
        for parity in range(n_par):
            column, exists = side_of(parity, col, n_cols, tile_cols)
            z = lateral(side_refs[parity][...]) * exists
            for t in range(tile_rows):
                put(flat, t, column, width, z[t * CW : (t + 1) * CW])

    for j in range(half + HA):
        gather(lat.at[0], j + (half - HA) * date, cat_a, j + date, width, -CW, width)
    for j in range(half + HB):
        gather(lat.at[1], j + (half - HB) * date, cat_b, j + date, width, -CW, width)
    pairs_a, pairs_b = half // 2, half // 2 + MO // 2
    z = conv([(cat_a, 1, pairs_a), (cat_b, 1, pairs_b)], w_fpn).astype(BF16)
    for i in range(2 * pairs_a):
        pyr_a[i + 4 * (1 - date)] = line_of(z, i, width)
    pyr_b[:CW] = jnp.zeros((CW, chans), F32)
    pyr_b[pyr_b.shape[0] - CW :] = jnp.zeros((CW, chans), F32)
    for i in range(2 * pairs_b):
        put(pyr_b, i + (4 + MO) * (1 - date), -CW, width, line_of(z, 2 * pairs_a + i, width).astype(F32))

    tiles = tile_columns(row, col, row >= 0, shift, n_cols, tile_cols, chans)
    inside = grid_columns(col, n_cols, tile_cols, chans)
    for i in range(4):
        y = i + half * (1 - date)
        keep_line = in_grid(first_half * half + y - 2, n_rows, tile_rows)
        value = difference(
            pyr_a[y], pyr_b, lambda sy, y=y: y - 2 - sy, [(tiles, None)], inside, keep_line, width
        )
        put(dif, i, -CW, width, value)
    for i in range(4):
        gather(dif, i, cat_d, i, width, -CW, width)
    z = conv([(cat_d, 0, 1)], w_dec1, 1)
    z = jnp.maximum(z + jnp.concatenate([b_dec1[...]] * 2, 1), 0.0)
    for i in range(2):
        keep_line = in_grid(first_half * half + i + half * (1 - date) - 1, n_rows, tile_rows)
        put(hid, i, -CW, width, on_grid(line_of(z, i, width), inside, keep_line))


def outer_body(n_par, n_rows, n_cols, tile_rows, tile_cols, shift, v_ref, *refs):
    corners = refs[:n_par]
    (_, _, t_a, t_b, t_d, t_h, w_lat, b_lat, w_fpn, w_dec1, b_dec1, w_dec2, b_dec2, w_out, b_out,
     out_ref, pyr_a, pyr_b, lat, cat_a, cat_b, dif, cat_d, hid, cat_h) = refs[n_par:]
    row, col, date = position()
    half, width, chans = tile_rows // 2, tile_cols + 2 * CW, w_lat.shape[-1]
    first_half = row * 2 + date
    has_row = jnp.where(date == 0, row > 0, row < n_rows - 1)
    row_keep = has_row.astype(F32)
    weight, bias = w_lat[...], b_lat[...]

    def lateral(x):
        return jnp.dot(x.reshape(-1, chans), weight, preferred_element_type=F32) + bias

    z = lateral(v_ref[...]) * row_keep
    for i in range(HA + HB):
        put(lat, i, 0, width, z[i * tile_cols : (i + 1) * tile_cols])
    if n_cols == 2:
        blank_side(lat, HA + HB, col, tile_cols, width)
    for parity in range(n_par):
        column, exists = side_of(parity, col, n_cols, tile_cols)
        z = lateral(corners[parity][...]) * (exists * row_keep)
        for i in range(HA + HB):
            put(lat, i, column, width, z[i * CW : (i + 1) * CW])
    for i in range(3):
        cat_a[i + HA * (1 - date)] = t_a[i + (half + 1) * date]
        cat_b[i + HB * (1 - date)] = t_b[i + (half + MO + 1) * date]
    for i in range(HA):
        gather(lat, i, cat_a, i + 3 * date, width, -CW, width)
    for i in range(HB):
        gather(lat, i + HA, cat_b, i + 3 * date, width, -CW, width)
    pairs_b = 2 + MO // 2
    z = conv([(cat_a, 0, 2), (cat_b, 0, pairs_b)], w_fpn).astype(BF16)
    for i in range(4):
        pyr_a[i + half * date] = line_of(z, i, width)
    for i in range(2 * pairs_b):
        put(pyr_b, i + (half + MO) * date, -CW, width, line_of(z, 4 + i, width).astype(F32))

    near_row = jnp.clip(row + jnp.where(date == 0, -1, 1), 0, n_rows - 1)
    tiles = tile_columns(row, col, row >= 0, shift, n_cols, tile_cols, chans)
    near = tile_columns(near_row, col, has_row, shift, n_cols, tile_cols, chans)
    inside = grid_columns(col, n_cols, tile_cols, chans)
    for i in range(half):
        y = jnp.where(date == 0, i, half + 3 - i)
        q_of = lambda sy, y=y: y - 2 - sy

        def is_own(sy, q_of=q_of):
            return jnp.where(date == 0, q_of(sy) >= 0, q_of(sy) < half).astype(F32)

        def is_near(sy, is_own=is_own):
            return 1.0 - is_own(sy)

        groups = [(tiles, is_own), (near, is_near)] if i < 2 + MO else [(tiles, None)]
        keep_line = in_grid(first_half * half + y - 2, n_rows, tile_rows)
        value = difference(pyr_a[y], pyr_b, q_of, groups, inside, keep_line, width)
        put(dif, y - 4 * date, -CW, width, value)

    for i in range(2):
        cat_d[i + half * (1 - date)] = t_d[i + 2 * date]
        put(hid, i + half * (1 - date), -CW, width, t_h[pl.ds(CW + i * width, width)])
    for i in range(half):
        gather(dif, i, cat_d, i + 2 * date, width, -CW, width)
    z = conv([(cat_d, 0, half // 2)], w_dec1)
    z = jnp.maximum(z + jnp.concatenate([b_dec1[...]] * 2, 1), 0.0)
    for i in range(half):
        y = i + 2 * date
        line = first_half * half + y - 1
        put(hid, y, -CW, width, on_grid(line_of(z, i, width), inside, in_grid(line, n_rows, tile_rows)))
    for i in range(half + 2):
        gather(hid, i, cat_h, i, tile_cols, 0, width)
    z = conv([(cat_h, 0, half // 2)], w_dec2)
    z = jnp.maximum(z + jnp.concatenate([b_dec2[...]] * 2, 1), 0.0).astype(BF16)
    none = jnp.zeros((1, chans), BF16)
    upper = jnp.concatenate([w_out[...], none], axis=1)
    lower = jnp.concatenate([none, w_out[...]], axis=1)
    weight = jnp.concatenate([upper, lower] * 8, axis=0)
    logit = lax.dot_general(weight, z, (((1,), (1,)), ((), ())), preferred_element_type=F32)
    for i in range(half // 2):
        out_ref[2 * i : 2 * i + 2] = logit[:2, i * tile_cols : (i + 1) * tile_cols] + b_out[...]


def fetch_body(n_par, tile_rows, tile_cols, x_hbm, rows, *refs):
    edges, sems = refs[:n_par], refs[n_par]
    _, col, date = position()
    parts = [(x_hbm.at[pl.ds((tile_rows - HB) * date, HB)], rows)]
    for p in range(n_par):
        column = pl.multiple_of(jnp.where(col % 2 == p, tile_cols - CW, 0), 8)
        parts.append((x_hbm.at[:, pl.ds(column, CW)], edges[p]))
    copies = [pltpu.make_async_copy(a, b, sems.at[k]) for k, (a, b) in enumerate(parts)]
    for copy in copies[::-1]:
        copy.start()
    for copy in copies:
        copy.wait()


def per_device(
    sizes, features, scene_shift, w_lat, b_lat, w_fpn, w_dec1, b_dec1, w_dec2, b_dec2, w_out, b_out
):
    _, n_rows, n_cols, _ = sizes
    tile_rows, tile_cols, chans = features.shape[1:]
    col, date = lax.axis_index("cols"), lax.axis_index("date")
    half, width = tile_rows // 2, tile_cols + 2 * CW
    n_par = 1 if n_cols == 2 else 2
    own = features[0]
    tile = pltpu.with_memory_space_constraint(own, pltpu.HBM)
    vmem = pl.BlockSpec(memory_space=pltpu.VMEM)
    kind = lambda *shape: jax.ShapeDtypeStruct(shape + (chans,), BF16)
    rows_own, *edges = pl.pallas_call(
        functools.partial(fetch_body, n_par, tile_rows, tile_cols),
        out_shape=(kind(HB, tile_cols),) + (kind(tile_rows, CW),) * n_par,
        in_specs=[pl.BlockSpec(memory_space=pltpu.HBM)],
        out_specs=(vmem,) * (1 + n_par),
        scratch_shapes=[pltpu.SemaphoreType.DMA((1 + n_par,))],
        compiler_params=pltpu.CompilerParams(vmem_limit_bytes=4 * 2**20),
        name="fetch",
    )(tile)
    first = date == 0

    def swap(value):
        return send(value, sizes, lambda r, c, d: (r, c, 1 - d))

    def edge(x, parity):
        return jnp.where(col % 2 == parity, x[:, tile_cols - CW :], x[:, :CW])

    def partner(c, parity):
        return column_partner(c, parity, n_cols)

    oth = swap(own)

    def shift_row(r, c, d):
        near = r - 1 + 2 * d
        return (near, c, 1 - d) if 0 <= near < n_rows else None

    def corner(p, r, c, d):
        near = shift_row(r, c, d)
        return None if near is None else (near[0], partner(c, p), near[2])

    mine, corners, others = [], [], []
    for p in range(n_par):
        mine.append(send(edges[p], sizes, lambda r, c, d, p=p: (r, partner(c, p), d)))
    rows_oth = lax.dynamic_slice_in_dim(oth, (tile_rows - HB) * date, HB, 0)
    for_row = jnp.concatenate(
        [
            jnp.where(first, rows_own[:HA], rows_oth[HB - HA :]),
            jnp.where(first, rows_oth, rows_own),
        ],
        axis=0,
    )
    from_row = send(for_row, sizes, shift_row)
    for p in range(n_par):
        others.append(swap(mine[p]))
    for p in range(n_par):
        corners.append(send(edge(for_row, p), sizes, functools.partial(corner, p)))
    smem = pl.BlockSpec(memory_space=pltpu.SMEM)
    lines_a, lines_b = half + 4, half + 4 + 2 * MO

    def flat(lines, kind=F32):
        return jax.ShapeDtypeStruct((2 * CW + lines * width, chans), kind)

    def cat(lines, columns=width):
        return jax.ShapeDtypeStruct((lines, 3, columns, chans), BF16)

    def scratch(shape):
        return pltpu.VMEM(shape.shape, shape.dtype)

    row_a = jax.ShapeDtypeStruct((lines_a, width, chans), BF16)
    lat_tile = flat(tile_rows)
    pyr_a, pyr_b, *kept = pl.pallas_call(
        functools.partial(inner_body, n_par, n_rows, n_cols, tile_rows, tile_cols),
        out_shape=(row_a, flat(lines_b), cat(half + HA + 1), cat(half + HB + 1), cat(4), flat(2)),
        in_specs=[smem] + [vmem] * (2 + 2 * n_par + 5),
        out_specs=(vmem,) * 6,
        scratch_shapes=[pltpu.VMEM((2,) + lat_tile.shape, F32), scratch(flat(4))],
        compiler_params=pltpu.CompilerParams(vmem_limit_bytes=24 * 2**20),
        cost_estimate=pl.CostEstimate(
            flops=2 * 10 * width * 1536 * 256, bytes_accessed=8 * 2**20, transcendentals=0
        ),
        name="inner",
    )(scene_shift, own, oth, *mine, *others, w_lat, b_lat[None], w_fpn, w_dec1, b_dec1[None])
    out, _, _ = pl.pallas_call(
        functools.partial(outer_body, n_par, n_rows, n_cols, tile_rows, tile_cols),
        out_shape=(jax.ShapeDtypeStruct((half, tile_cols), F32), row_a, flat(lines_b)),
        in_specs=[smem] + [vmem] * (n_par + 1 + 15),
        out_specs=(vmem,) * 3,
        input_output_aliases={n_par + 2: 1, n_par + 3: 2},
        scratch_shapes=[
            scratch(flat(HA + HB)),
            scratch(cat(HA + 3)),
            scratch(cat(HB + 3)),
            scratch(flat(half)),
            scratch(cat(half + 2)),
            scratch(flat(half + 2)),
            scratch(cat(half + 2, tile_cols)),
        ],
        compiler_params=pltpu.CompilerParams(vmem_limit_bytes=24 * 2**20),
        name="outer",
    )(
        scene_shift, from_row, *corners, pyr_a, pyr_b, *kept,
        w_lat, b_lat[None], w_fpn, w_dec1, b_dec1[None], w_dec2, b_dec2[None], w_out[None], jnp.broadcast_to(b_out, (1, tile_cols)),
    )
    return out


def staged(sizes, *args):
    return per_device(sizes, *args)


def solution(mesh):
    sizes = tuple(mesh.shape[axis] for axis in ("groups", "rows", "cols", "date"))
    return jax.shard_map(
        functools.partial(staged, sizes),
        mesh=mesh,
        in_specs=(P("date", ("groups", "rows"), "cols", None), P("groups", None, None)) + (P(),) * 9,
        out_specs=P(("groups", "rows", "date"), "cols"),
        check_vma=False,
    )
```

```python
import functools

import jax
import jax.numpy as jnp
from jax import lax
from jax.experimental import pallas as pl
from jax.experimental.pallas import tpu as pltpu
from jax.sharding import PartitionSpec as P


MO = 4
HA = 3
HB = HA + MO
CW = 8
STRIP = 16
F32 = jnp.float32
BF16 = jnp.bfloat16


def column_partner(col, parity, n_cols):
    right = col % 2 == parity
    return (col + 1) % n_cols if right else (col - 1) % n_cols


def send(value, sizes, target):
    n_groups, n_rows, n_cols, n_dates = sizes

    def place(group, row, col, date):
        return ((group * n_rows + row) * n_cols + col) * n_dates + date

    pairs = []
    for group in range(n_groups):
        for row in range(n_rows):
            for col in range(n_cols):
                for date in range(n_dates):
                    to = target(row, col, date)
                    end = (
                        place((group + 1) % n_groups, row, col, date)
                        if to is None
                        else place(group, *to)
                    )
                    pairs.append((place(group, row, col, date), end))
    return lax.ppermute(value, ("groups", "rows", "cols", "date"), pairs)


def at(line, column, width):
    return CW + line * width + CW + column


def position():
    return lax.axis_index("rows"), lax.axis_index("cols"), lax.axis_index("date")


def put(target, line, column, width, value):
    start = at(line, column, width)
    target[start : start + value.shape[0]] = value


def gather(source, line, cat, index, count, column, width):
    start = at(line, column, width)
    for tap in range(3):
        cat[index, tap] = source[start + tap - 1 : start + tap - 1 + count].astype(BF16)


def conv(parts, w_ref, date, ways=2):
    taps = [w_ref[a + (2 - 2 * a) * date].reshape(-1, w_ref.shape[-1]) for a in range(3)]
    none = jnp.zeros_like(taps[0])
    tall = jnp.concatenate(
        [jnp.concatenate(taps + [none], axis=0), jnp.concatenate([none] + taps, axis=0)], axis=1
    )
    tops = [(cat, first + 2 * i) for cat, first, pairs in parts for i in range(pairs)]
    outs = []
    for way in range(ways):
        some = tops[way * len(tops) // ways : (way + 1) * len(tops) // ways]
        lines = [
            jnp.concatenate([cat[top + j, tap] for cat, top in some], axis=0)
            for j in range(4)
            for tap in range(3)
        ]
        outs.append(jnp.dot(jnp.concatenate(lines, axis=1), tall, preferred_element_type=F32))
    return jnp.concatenate(outs, axis=0)


def line_of(z, index, columns):
    chans = z.shape[1] // 2
    pair, k = divmod(index, 2)
    return z[pair * columns : (pair + 1) * columns, k * chans : (k + 1) * chans]


def put_sides(lat, line, col, n_cols, tile_cols, width, halves):
    even = col % 2 == 0
    right = halves[0] * (even & (col < n_cols - 1)).astype(F32)
    left = halves[0] * (~even).astype(F32)
    if len(halves) == 2:
        right = right + halves[1] * (~even & (col < n_cols - 1)).astype(F32)
        left = left + halves[1] * (even & (col > 0)).astype(F32)
    put(lat, line, -CW, width, left)
    put(lat, line, tile_cols, width, right)


def tile_columns(row, col, there, shift, date, n_cols, tile_cols, chans):
    cells = lax.broadcasted_iota(jnp.int32, (STRIP, chans), 0)
    tiles = []
    for step in (0, -1, 1):
        c = jnp.clip(col + step, 0, n_cols - 1)
        is_tile = (there & (col + step >= 0) & (col + step < n_cols)).astype(F32)
        sy, sx = shift[row, c, 0] * (1 - 2 * date), shift[row, c, 1]
        low = sx + step * tile_cols
        masks = []
        for left in (True, False):
            x = cells + (-CW if left else tile_cols + CW - STRIP)
            masks.append(((x >= low) & (x < low + tile_cols)).astype(F32) * is_tile)
        tiles.append((sy, sx, is_tile, masks[0], masks[1]))
    return tiles


def shares(count):
    share = jnp.where(count > 1.5, 0.5, 1.0)
    share = jnp.where(count > 2.5, 1.0 / 3.0, share)
    return jnp.where(count > 3.5, 0.25, share)


def difference(a_line, pyr_b, u, groups, inside, keep_line, width):
    plus = lambda x, y: y if x is None else x + y
    count = [None, None]
    level = [None, None]
    mids = []
    for tiles, hit_of in groups:
        for k, (sy, sx, is_tile, *masks) in enumerate(tiles):
            start = CW + (u - sy + 2 + MO) * width - sx
            hit = None if hit_of is None else hit_of(sy)
            for side in range(2):
                if k != 2 - side:
                    mask = masks[side] if hit is None else masks[side] * hit
                    count[side] = plus(count[side], mask)
                    strip = pyr_b[pl.ds(start + side * (width - STRIP), STRIP)] * mask
                    level[side] = plus(level[side], strip)
            if k == 0:
                value = pyr_b[pl.ds(start + STRIP, width - 2 * STRIP)]
                mids.append((value, None if hit is None else hit * is_tile))
    a = a_line.astype(F32)
    outs = []
    for side in range(2):
        part = a[:STRIP] if side == 0 else a[width - STRIP :]
        value = jnp.abs(part - level[side] * shares(count[side]))
        keep = jnp.minimum(count[side], 1.0) * inside[side]
        outs.append(value * (keep if keep_line is None else keep * keep_line))
    middle = a[STRIP : width - STRIP]
    if len(mids) == 1:
        middle = jnp.abs(middle - mids[0][0])
    else:
        weight = mids[0][1] + mids[1][1]
        share = jnp.where(weight > 1.5, 0.5, 1.0)
        keep = jnp.minimum(weight, 1.0)
        keep = keep if keep_line is None else keep * keep_line
        total = mids[0][0] * (mids[0][1] * share) + mids[1][0] * (mids[1][1] * share)
        middle = jnp.abs(middle - total) * keep
    return jnp.concatenate([outs[0], middle, outs[1]], axis=0)


def grid_columns(col, n_cols, tile_cols, chans):
    x = lax.broadcasted_iota(jnp.int32, (STRIP, chans), 0) + col * tile_cols
    return [
        ((x + at >= 0) & (x + at < n_cols * tile_cols)).astype(F32)
        for at in (-CW, tile_cols + CW - STRIP)
    ]


def on_grid(line, inside, keep_line):
    parts = [line[:STRIP] * inside[0], line[STRIP:-STRIP], line[-STRIP:] * inside[1]]
    if keep_line is not None:
        parts = [part * keep_line for part in parts]
    return jnp.concatenate(parts, axis=0)


def inner_body(n_par, n_cols, tile_rows, tile_cols, shift, own, oth, *refs):
    mine, others = refs[:n_par], refs[n_par : 2 * n_par]
    (w_lat, b_lat, w_fpn, w_dec1, b_dec1,
     pyr_a, pyr_b, t_a, t_b, t_d, hid, lat_a, lat_b, cat_a, cat_b, cat_d, dif) = refs[2 * n_par :]
    row, col, date = position()
    half, width, chans = tile_rows // 2, tile_cols + 2 * CW, own.shape[-1]
    weight, bias = w_lat[...], b_lat[...]

    def lateral(x):
        return jnp.dot(x, weight, preferred_element_type=F32) + bias

    for lat, cat, lines, is_own in (
        (lat_a, cat_a, half + HA, date == 0),
        (lat_b, cat_b, half + HB, date == 1),
    ):
        rows = [u + (tile_rows - 1 - 2 * u) * date for u in range(lines)]

        def pick(x, y, is_own=is_own):
            return jnp.where(is_own, x, y)

        z = lateral(jnp.concatenate([pick(own[t], oth[t]) for t in rows], axis=0))
        for u in range(lines):
            put(lat, u, 0, width, z[u * tile_cols : (u + 1) * tile_cols])
        z = [
            lateral(jnp.concatenate([pick(mine[p][t], others[p][t]) for t in rows], axis=0))
            for p in range(n_par)
        ]
        for u in range(lines):
            put_sides(lat, u, col, n_cols, tile_cols, width, [x[u * CW : (u + 1) * CW] for x in z])
        for u in range(lines):
            gather(lat, u, cat, u, width, -CW, width)
    for u in range(3):
        t_a[u] = cat_a[u]
        t_b[u] = cat_b[u]
    pairs_a, pairs_b = half // 2, half // 2 + MO // 2
    z = conv([(cat_a, 1, pairs_a), (cat_b, 1, pairs_b)], w_fpn, date).astype(BF16)
    for i in range(2 * pairs_a):
        pyr_a[i] = line_of(z, i, width)
    pyr_b[:CW] = jnp.zeros((CW, chans), F32)
    pyr_b[pyr_b.shape[0] - CW :] = jnp.zeros((CW, chans), F32)
    for i in range(2 * pairs_b):
        put(pyr_b, i + 4 + MO, -CW, width, line_of(z, 2 * pairs_a + i, width).astype(F32))

    tiles = tile_columns(row, col, row >= 0, shift, date, n_cols, tile_cols, chans)
    inside = grid_columns(col, n_cols, tile_cols, chans)
    for i in range(4):
        u = i + half - 2
        value = difference(pyr_a[u - 2], pyr_b, u, [(tiles, None)], inside, None, width)
        put(dif, i, -CW, width, value)
    for i in range(4):
        gather(dif, i, cat_d, i, width, -CW, width)
    for i in range(2):
        t_d[i] = cat_d[i]
    z = conv([(cat_d, 0, 1)], w_dec1, date, 1)
    z = jnp.maximum(z + jnp.concatenate([b_dec1[...]] * 2, 1), 0.0)
    for i in range(2):
        put(hid, i, -CW, width, on_grid(line_of(z, i, width), inside, None))


def outer_body(n_par, n_rows, n_cols, tile_rows, tile_cols, shift, v_ref, *refs):
    corners = refs[:n_par]
    (in_a, _, t_a, t_b, t_d, t_h, w_lat, b_lat, w_fpn, w_dec1, b_dec1, w_dec2, b_dec2, w_out, b_out,
     out_ref, pyr_b, pyr_a, lat, cat_a, cat_b, dif, cat_d, hid, cat_h) = refs[n_par:]
    row, col, date = position()
    half, width, chans = tile_rows // 2, tile_cols + 2 * CW, w_lat.shape[-1]
    has_row = jnp.where(date == 0, row > 0, row < n_rows - 1)
    row_keep = has_row.astype(F32)
    weight, bias = w_lat[...], b_lat[...]

    def lateral(x):
        return (jnp.dot(x, weight, preferred_element_type=F32) + bias) * row_keep

    lines = [i + (HA - 1 - 2 * i) * date for i in range(HA)]
    lines += [HA + i + (HB - 1 - 2 * i) * date for i in range(HB)]
    z = lateral(jnp.concatenate([v_ref[i] for i in lines], axis=0))
    for i in range(HA + HB):
        put(lat, i, 0, width, z[i * tile_cols : (i + 1) * tile_cols])
    z = [lateral(jnp.concatenate([corners[p][i] for i in lines], axis=0)) for p in range(n_par)]
    for i in range(HA + HB):
        put_sides(lat, i, col, n_cols, tile_cols, width, [x[i * CW : (i + 1) * CW] for x in z])
    for i in range(HA):
        gather(lat, i, cat_a, i, width, -CW, width)
    for i in range(HB):
        gather(lat, i + HA, cat_b, i, width, -CW, width)
    for i in range(3):
        cat_a[i + HA] = t_a[i]
        cat_b[i + HB] = t_b[i]
    pairs_b = 2 + MO // 2
    z = conv([(cat_a, 0, 2), (cat_b, 0, pairs_b)], w_fpn, date).astype(BF16)
    for i in range(4):
        pyr_a[i] = line_of(z, i, width)
    for i in range(2 * pairs_b):
        put(pyr_b, i, -CW, width, line_of(z, 4 + i, width).astype(F32))

    near_row = jnp.clip(row + jnp.where(date == 0, -1, 1), 0, n_rows - 1)
    tiles = tile_columns(row, col, row >= 0, shift, date, n_cols, tile_cols, chans)
    near = tile_columns(near_row, col, has_row, shift, date, n_cols, tile_cols, chans)
    inside = grid_columns(col, n_cols, tile_cols, chans)
    for i in range(half):
        u = i - 2
        groups = [(tiles, None)]
        if u < MO:
            groups = [
                (tiles, lambda sy, u=u: (u - sy >= 0).astype(F32)),
                (near, lambda sy, u=u: (u - sy < 0).astype(F32)),
            ]
        a_line = pyr_a[u + 2] if u < 2 else in_a[u - 2]
        value = difference(a_line, pyr_b, u, groups, inside, row_keep if u < 0 else None, width)
        put(dif, i, -CW, width, value)
    for i in range(half):
        gather(dif, i, cat_d, i, width, -CW, width)
    for i in range(2):
        cat_d[i + half] = t_d[i]
        put(hid, i + half, -CW, width, t_h[CW + i * width : CW + (i + 1) * width])
    z = conv([(cat_d, 0, half // 2)], w_dec1, date)
    z = jnp.maximum(z + jnp.concatenate([b_dec1[...]] * 2, 1), 0.0)
    for i in range(half):
        put(hid, i, -CW, width, on_grid(line_of(z, i, width), inside, None if i else row_keep))
    for i in range(half + 2):
        gather(hid, i, cat_h, i, tile_cols, 0, width)
    z = conv([(cat_h, 0, half // 2)], w_dec2, date)
    z = jnp.maximum(z + jnp.concatenate([b_dec2[...]] * 2, 1), 0.0).astype(BF16)
    none = jnp.zeros((1, chans), BF16)
    upper = jnp.concatenate([w_out[...], none], axis=1)
    lower = jnp.concatenate([none, w_out[...]], axis=1)
    weight = jnp.concatenate([upper, lower] * 8, axis=0)
    logit = lax.dot_general(weight, z, (((1,), (1,)), ((), ())), preferred_element_type=F32)
    for i in range(half):
        pair, k = divmod(i, 2)
        line = logit[k : k + 1, pair * tile_cols : (pair + 1) * tile_cols] + b_out[...]
        out_ref[pl.ds(i + (half - 1 - 2 * i) * date, 1)] = line


def fetch_body(n_par, tile_rows, tile_cols, x_hbm, rows, *refs):
    edges, sems = refs[:n_par], refs[n_par]
    _, col, date = position()
    parts = [(x_hbm.at[pl.ds((tile_rows - HB) * date, HB)], rows)]
    for p in range(n_par):
        column = pl.multiple_of(jnp.where(col % 2 == p, tile_cols - CW, 0), 8)
        parts.append((x_hbm.at[:, pl.ds(column, CW)], edges[p]))
    copies = [pltpu.make_async_copy(a, b, sems.at[k]) for k, (a, b) in enumerate(parts)]
    for copy in copies[::-1]:
        copy.start()
    for copy in copies:
        copy.wait()


def per_device(
    sizes, features, scene_shift, w_lat, b_lat, w_fpn, w_dec1, b_dec1, w_dec2, b_dec2, w_out, b_out
):
    _, n_rows, n_cols, _ = sizes
    tile_rows, tile_cols, chans = features.shape[1:]
    col, date = lax.axis_index("cols"), lax.axis_index("date")
    half, width = tile_rows // 2, tile_cols + 2 * CW
    n_par = 1 if n_cols == 2 else 2
    own = features[0]
    tile = pltpu.with_memory_space_constraint(own, pltpu.HBM)
    vmem = pl.BlockSpec(memory_space=pltpu.VMEM)
    kind = lambda *shape: jax.ShapeDtypeStruct(shape + (chans,), BF16)
    rows_own, *edges = pl.pallas_call(
        functools.partial(fetch_body, n_par, tile_rows, tile_cols),
        out_shape=(kind(HB, tile_cols),) + (kind(tile_rows, CW),) * n_par,
        in_specs=[pl.BlockSpec(memory_space=pltpu.HBM)],
        out_specs=(vmem,) * (1 + n_par),
        scratch_shapes=[pltpu.SemaphoreType.DMA((1 + n_par,))],
        compiler_params=pltpu.CompilerParams(vmem_limit_bytes=4 * 2**20),
        name="fetch",
    )(tile)
    first = date == 0

    def swap(value):
        return send(value, sizes, lambda r, c, d: (r, c, 1 - d))

    def edge(x, parity):
        return jnp.where(col % 2 == parity, x[:, tile_cols - CW :], x[:, :CW])

    def partner(c, parity):
        return column_partner(c, parity, n_cols)

    oth = swap(own)

    def shift_row(r, c, d):
        near = r - 1 + 2 * d
        return (near, c, 1 - d) if 0 <= near < n_rows else None

    def corner(p, r, c, d):
        near = shift_row(r, c, d)
        return None if near is None else (near[0], partner(c, p), near[2])

    mine, corners, others = [], [], []
    for p in range(n_par):
        mine.append(send(edges[p], sizes, lambda r, c, d, p=p: (r, partner(c, p), d)))
    rows_oth = lax.dynamic_slice_in_dim(oth, (tile_rows - HB) * date, HB, 0)
    for_row = jnp.concatenate(
        [
            jnp.where(first, rows_own[:HA], rows_oth[HB - HA :]),
            jnp.where(first, rows_oth, rows_own),
        ],
        axis=0,
    )
    from_row = send(for_row, sizes, shift_row)
    for p in range(n_par):
        others.append(swap(mine[p]))
    for p in range(n_par):
        corners.append(send(edge(for_row, p), sizes, functools.partial(corner, p)))
    smem = pl.BlockSpec(memory_space=pltpu.SMEM)
    lines_b = half + 4 + 2 * MO

    def flat(lines, kind=F32):
        return jax.ShapeDtypeStruct((2 * CW + lines * width, chans), kind)

    def cat(lines, columns=width):
        return jax.ShapeDtypeStruct((lines, 3, columns, chans), BF16)

    def scratch(shape):
        return pltpu.VMEM(shape.shape, shape.dtype)

    def lines_of(lines):
        return jax.ShapeDtypeStruct((lines, width, chans), BF16)

    pyr_a, pyr_b, *kept = pl.pallas_call(
        functools.partial(inner_body, n_par, n_cols, tile_rows, tile_cols),
        out_shape=(lines_of(half), flat(lines_b), cat(3), cat(3), cat(2), flat(2)),
        in_specs=[smem] + [vmem] * (2 + 2 * n_par + 5),
        out_specs=(vmem,) * 6,
        scratch_shapes=[
            scratch(flat(half + HA)),
            scratch(flat(half + HB)),
            scratch(cat(half + HA)),
            scratch(cat(half + HB)),
            scratch(cat(4)),
            scratch(flat(4)),
        ],
        compiler_params=pltpu.CompilerParams(vmem_limit_bytes=28 * 2**20),
        cost_estimate=pl.CostEstimate(
            flops=2 * 10 * width * 1536 * 256, bytes_accessed=8 * 2**20, transcendentals=0
        ),
        name="inner",
    )(scene_shift, own, oth, *mine, *others, w_lat, b_lat[None], w_fpn, w_dec1, b_dec1[None])
    out, _ = pl.pallas_call(
        functools.partial(outer_body, n_par, n_rows, n_cols, tile_rows, tile_cols),
        out_shape=(jax.ShapeDtypeStruct((half, tile_cols), F32), flat(lines_b)),
        in_specs=[smem] + [vmem] * (n_par + 1 + 15),
        out_specs=(vmem,) * 2,
        input_output_aliases={n_par + 3: 1},
        scratch_shapes=[
            scratch(lines_of(4)),
            scratch(flat(HA + HB)),
            scratch(cat(HA + 3)),
            scratch(cat(HB + 3)),
            scratch(flat(half)),
            scratch(cat(half + 2)),
            scratch(flat(half + 2)),
            scratch(cat(half + 2, tile_cols)),
        ],
        compiler_params=pltpu.CompilerParams(vmem_limit_bytes=24 * 2**20),
        name="outer",
    )(
        scene_shift, from_row, *corners, pyr_a, pyr_b, *kept,
        w_lat, b_lat[None], w_fpn, w_dec1, b_dec1[None], w_dec2, b_dec2[None], w_out[None],
        jnp.broadcast_to(b_out, (1, tile_cols)),
    )
    return out


def staged(sizes, *args):
    return per_device(sizes, *args)


def solution(mesh):
    sizes = tuple(mesh.shape[axis] for axis in ("groups", "rows", "cols", "date"))
    return jax.shard_map(
        functools.partial(staged, sizes),
        mesh=mesh,
        in_specs=(P("date", ("groups", "rows"), "cols", None), P("groups", None, None)) + (P(),) * 9,
        out_specs=P(("groups", "rows", "date"), "cols"),
        check_vma=False,
    )
```

```python
import functools

import jax
import jax.numpy as jnp
from jax import lax
from jax.experimental import pallas as pl
from jax.experimental.pallas import tpu as pltpu
from jax.sharding import PartitionSpec as P


MO = 4
HA = 3
HB = HA + MO
CW = 8
STRIP = 16
F32 = jnp.float32
BF16 = jnp.bfloat16


def column_partner(col, parity, n_cols):
    right = col % 2 == parity
    return (col + 1) % n_cols if right else (col - 1) % n_cols


def send(value, sizes, target):
    n_groups, n_rows, n_cols, n_dates = sizes

    def place(group, row, col, date):
        return ((group * n_rows + row) * n_cols + col) * n_dates + date

    pairs = []
    for group in range(n_groups):
        for row in range(n_rows):
            for col in range(n_cols):
                for date in range(n_dates):
                    to = target(row, col, date)
                    end = (
                        place((group + 1) % n_groups, row, col, date)
                        if to is None
                        else place(group, *to)
                    )
                    pairs.append((place(group, row, col, date), end))
    return lax.ppermute(value, ("groups", "rows", "cols", "date"), pairs)


def at(line, column, width):
    return CW + line * width + CW + column


def position():
    return lax.axis_index("rows"), lax.axis_index("cols"), lax.axis_index("date")


def put(target, line, column, width, value):
    start = at(line, column, width)
    target[start : start + value.shape[0]] = value


def gather(source, line, cat, index, count, column, width):
    start = at(line, column, width)
    for tap in range(3):
        cat[index, tap] = source[start + tap - 1 : start + tap - 1 + count].astype(BF16)


def conv(groups, w_ref, date, ways=2):
    taps = [w_ref[a + (2 - 2 * a) * date].reshape(-1, w_ref.shape[-1]) for a in range(3)]
    none = jnp.zeros_like(taps[0])
    tall = jnp.concatenate(
        [jnp.concatenate(taps + [none], axis=0), jnp.concatenate([none] + taps, axis=0)], axis=1
    )
    pairs = [lines[top : top + 4] for lines in groups for top in range(0, len(lines) - 2, 2)]
    outs = []
    for way in range(ways):
        some = pairs[way * len(pairs) // ways : (way + 1) * len(pairs) // ways]
        lines = [
            jnp.concatenate([pair[j][0][pair[j][1], tap] for pair in some], axis=0)
            for j in range(4)
            for tap in range(3)
        ]
        outs.append(jnp.dot(jnp.concatenate(lines, axis=1), tall, preferred_element_type=F32))
    return jnp.concatenate(outs, axis=0)


def run(cat, first, count):
    return [(cat, first + i) for i in range(count)]


def line_of(z, index, columns):
    chans = z.shape[1] // 2
    pair, k = divmod(index, 2)
    return z[pair * columns : (pair + 1) * columns, k * chans : (k + 1) * chans]


def put_sides(lat, line, col, n_cols, tile_cols, width, halves):
    even = col % 2 == 0
    right = halves[0] * (even & (col < n_cols - 1)).astype(F32)
    left = halves[0] * (~even).astype(F32)
    if len(halves) == 2:
        right = right + halves[1] * (~even & (col < n_cols - 1)).astype(F32)
        left = left + halves[1] * (even & (col > 0)).astype(F32)
    put(lat, line, -CW, width, left)
    put(lat, line, tile_cols, width, right)


def tile_columns(row, col, there, shift, date, n_cols, tile_cols, chans):
    cells = lax.broadcasted_iota(jnp.int32, (STRIP, chans), 0)
    tiles = []
    for step in (0, -1, 1):
        c = jnp.clip(col + step, 0, n_cols - 1)
        is_tile = (there & (col + step >= 0) & (col + step < n_cols)).astype(F32)
        sy, sx = shift[row, c, 0] * (1 - 2 * date), shift[row, c, 1]
        low = sx + step * tile_cols
        masks = []
        for left in (True, False):
            x = cells + (-CW if left else tile_cols + CW - STRIP)
            masks.append(((x >= low) & (x < low + tile_cols)).astype(F32) * is_tile)
        tiles.append((sy, sx, is_tile, masks[0], masks[1]))
    return tiles


def shares(count):
    share = jnp.where(count > 1.5, 0.5, 1.0)
    share = jnp.where(count > 2.5, 1.0 / 3.0, share)
    return jnp.where(count > 3.5, 0.25, share)


def difference(a_line, pyr_b, u, groups, inside, keep_line, width):
    plus = lambda x, y: y if x is None else x + y
    blank = pyr_b.shape[0] - CW - width
    count = [None, None]
    level = [None, None]
    middle, weight = None, 0.0
    for tiles, hit_of in groups:
        for k, (sy, sx, is_tile, *masks) in enumerate(tiles):
            start = CW + (u - sy + 2 + MO) * width - sx
            hit = None
            if hit_of is not None:
                hit = hit_of(sy).astype(F32)
                start = jnp.where(hit_of(sy), start, blank)
            for side in range(2):
                if k != 2 - side:
                    mask = masks[side] if hit is None else masks[side] * hit
                    count[side] = plus(count[side], mask)
                    strip = pyr_b[pl.ds(start + side * (width - STRIP), STRIP)] * masks[side]
                    level[side] = plus(level[side], strip)
            if k == 0:
                if hit is not None:
                    weight = weight + hit * is_tile
                    start = jnp.where(is_tile > 0, start, blank)
                middle = plus(middle, pyr_b[pl.ds(start + STRIP, width - 2 * STRIP)])
    outs = []
    for side in range(2):
        part = a_line[:STRIP] if side == 0 else a_line[width - STRIP :]
        value = jnp.abs(part - level[side] * shares(count[side]))
        keep = jnp.minimum(count[side], 1.0) * inside[side]
        outs.append(value * (keep if keep_line is None else keep * keep_line))
    part = a_line[STRIP : width - STRIP]
    if len(groups) == 1:
        middle = jnp.abs(part - middle)
    else:
        keep = jnp.minimum(weight, 1.0)
        keep = keep if keep_line is None else keep * keep_line
        middle = jnp.abs(part - middle * jnp.where(weight > 1.5, 0.5, 1.0)) * keep
    return jnp.concatenate([outs[0], middle, outs[1]], axis=0)


def grid_columns(col, n_cols, tile_cols, chans):
    x = lax.broadcasted_iota(jnp.int32, (STRIP, chans), 0) + col * tile_cols
    return [
        ((x + at >= 0) & (x + at < n_cols * tile_cols)).astype(F32)
        for at in (-CW, tile_cols + CW - STRIP)
    ]


def on_grid(line, inside, keep_line):
    parts = [line[:STRIP] * inside[0], line[STRIP:-STRIP], line[-STRIP:] * inside[1]]
    if keep_line is not None:
        parts = [part * keep_line for part in parts]
    return jnp.concatenate(parts, axis=0)


def inner_body(n_par, n_cols, tile_rows, tile_cols, shift_in, own, oth, *refs):
    mine, others = refs[:n_par], refs[n_par : 2 * n_par]
    (w_lat, b_lat, w_fpn, w_dec1, b_dec1,
     pyr_a, pyr_b, t_a, t_b, t_d, hid, lat_a, lat_b, cat_a, cat_b, cat_d, dif, shift, sem) = refs[2 * n_par :]
    shift_copy = pltpu.make_async_copy(shift_in, shift, sem)
    shift_copy.start()
    row, col, date = position()
    half, width, chans = tile_rows // 2, tile_cols + 2 * CW, own.shape[-1]
    weight, bias = w_lat[...], b_lat[...]

    def lateral(x):
        return jnp.dot(x, weight, preferred_element_type=F32) + bias

    for lat, cat, lines, is_own in (
        (lat_a, cat_a, half + HA, date == 0),
        (lat_b, cat_b, half + HB, date == 1),
    ):
        rows = [u + (tile_rows - 1 - 2 * u) * date for u in range(lines)]

        def pick(x, y, is_own=is_own):
            return jnp.where(is_own, x, y)

        z = lateral(jnp.concatenate([pick(own[t], oth[t]) for t in rows], axis=0))
        for u in range(lines):
            put(lat, u, 0, width, z[u * tile_cols : (u + 1) * tile_cols])
        z = [
            lateral(jnp.concatenate([pick(mine[p][t], others[p][t]) for t in rows], axis=0))
            for p in range(n_par)
        ]
        for u in range(lines):
            put_sides(lat, u, col, n_cols, tile_cols, width, [x[u * CW : (u + 1) * CW] for x in z])
        for u in range(lines):
            gather(lat, u, cat, u, width, -CW, width)
    for u in range(3):
        t_a[u] = cat_a[u]
        t_b[u] = cat_b[u]
    pairs_a, pairs_b = half // 2, half // 2 + MO // 2
    z = conv([run(cat_a, 1, 2 * pairs_a + 2), run(cat_b, 1, 2 * pairs_b + 2)], w_fpn, date)
    for i in range(2 * pairs_a):
        pyr_a[i] = line_of(z, i, width)
    pyr_b[:CW] = jnp.zeros((CW, chans), F32)
    blank = pyr_b.shape[0] - CW - width
    pyr_b[blank:] = jnp.zeros((width + CW, chans), F32)
    for i in range(2 * pairs_b):
        put(pyr_b, i + 4 + MO, -CW, width, line_of(z, 2 * pairs_a + i, width))

    shift_copy.wait()
    tiles = tile_columns(row, col, row >= 0, shift, date, n_cols, tile_cols, chans)
    inside = grid_columns(col, n_cols, tile_cols, chans)
    for i in range(4):
        u = i + half - 2
        value = difference(pyr_a[u - 2], pyr_b, u, [(tiles, None)], inside, None, width)
        put(dif, i, -CW, width, value)
    for i in range(4):
        gather(dif, i, cat_d, i, width, -CW, width)
    for i in range(2):
        t_d[i] = cat_d[i]
    z = conv([run(cat_d, 0, 4)], w_dec1, date, 1)
    z = jnp.maximum(z + jnp.concatenate([b_dec1[...]] * 2, 1), 0.0)
    for i in range(2):
        put(hid, i, -CW, width, on_grid(line_of(z, i, width), inside, None))


def outer_body(n_par, n_rows, n_cols, tile_rows, tile_cols, shift_in, v_ref, *refs):
    corners = refs[:n_par]
    (in_a, _, t_a, t_b, t_d, t_h, w_lat, b_lat, w_fpn, w_dec1, b_dec1, w_dec2, b_dec2, w_out, b_out,
     out_ref, pyr_b, pyr_a, lat, cat_a, cat_b, dif, cat_d, hid, cat_h, shift, sem) = refs[n_par:]
    shift_copy = pltpu.make_async_copy(shift_in, shift, sem)
    shift_copy.start()
    row, col, date = position()
    half, width, chans = tile_rows // 2, tile_cols + 2 * CW, w_lat.shape[-1]
    has_row = jnp.where(date == 0, row > 0, row < n_rows - 1)
    row_keep = has_row.astype(F32)
    weight, bias = jnp.where(has_row, w_lat[...], 0), b_lat[...] * row_keep

    def lateral(x):
        return jnp.dot(x, weight, preferred_element_type=F32) + bias

    lines = [i + (HA - 1 - 2 * i) * date for i in range(HA)]
    lines += [HA + i + (HB - 1 - 2 * i) * date for i in range(HB)]
    z = lateral(jnp.concatenate([v_ref[i] for i in lines], axis=0))
    for i in range(HA + HB):
        put(lat, i, 0, width, z[i * tile_cols : (i + 1) * tile_cols])
    z = [lateral(jnp.concatenate([corners[p][i] for i in lines], axis=0)) for p in range(n_par)]
    for i in range(HA + HB):
        put_sides(lat, i, col, n_cols, tile_cols, width, [x[i * CW : (i + 1) * CW] for x in z])
    for i in range(HA):
        gather(lat, i, cat_a, i, width, -CW, width)
    for i in range(HB):
        gather(lat, i + HA, cat_b, i, width, -CW, width)
    pairs_b = 2 + MO // 2
    z = conv([run(cat_a, 0, HA) + run(t_a, 0, 3), run(cat_b, 0, HB) + run(t_b, 0, 3)], w_fpn, date)
    for i in range(4):
        pyr_a[i] = line_of(z, i, width)
    for i in range(2 * pairs_b):
        put(pyr_b, i, -CW, width, line_of(z, 4 + i, width))

    near_row = jnp.clip(row + jnp.where(date == 0, -1, 1), 0, n_rows - 1)
    shift_copy.wait()
    tiles = tile_columns(row, col, row >= 0, shift, date, n_cols, tile_cols, chans)
    near = tile_columns(near_row, col, has_row, shift, date, n_cols, tile_cols, chans)
    inside = grid_columns(col, n_cols, tile_cols, chans)
    for i in range(half):
        u = i - 2
        groups = [(tiles, None)]
        if u < MO:
            groups = [
                (tiles, lambda sy, u=u: u - sy >= 0),
                (near, lambda sy, u=u: u - sy < 0),
            ]
        a_line = pyr_a[u + 2] if u < 2 else in_a[u - 2]
        value = difference(a_line, pyr_b, u, groups, inside, row_keep if u < 0 else None, width)
        put(dif, i, -CW, width, value)
    for i in range(half):
        gather(dif, i, cat_d, i, width, -CW, width)
    z = conv([run(cat_d, 0, half) + run(t_d, 0, 2)], w_dec1, date)
    z = jnp.maximum(z + jnp.concatenate([b_dec1[...]] * 2, 1), 0.0)
    for i in range(half):
        put(hid, i, -CW, width, on_grid(line_of(z, i, width), inside, None if i else row_keep))
    for i in range(half):
        gather(hid, i, cat_h, i, tile_cols, 0, width)
    for i in range(2):
        gather(t_h, i, cat_h, i + half, tile_cols, 0, width)
    z = conv([run(cat_h, 0, half + 2)], w_dec2, date)
    z = jnp.maximum(z + jnp.concatenate([b_dec2[...]] * 2, 1), 0.0).astype(BF16)
    none = jnp.zeros((1, chans), BF16)
    upper = jnp.concatenate([w_out[...], none], axis=1)
    lower = jnp.concatenate([none, w_out[...]], axis=1)
    weight = jnp.concatenate([upper, lower] * 8, axis=0)
    logit = lax.dot_general(weight, z, (((1,), (1,)), ((), ())), preferred_element_type=F32)
    for i in range(half):
        pair, k = divmod(i, 2)
        line = logit[k : k + 1, pair * tile_cols : (pair + 1) * tile_cols] + b_out[...]
        out_ref[pl.ds(i + (half - 1 - 2 * i) * date, 1)] = line


def fetch_body(n_par, tile_rows, tile_cols, x_hbm, rows, *refs):
    edges, sems = refs[:n_par], refs[n_par]
    _, col, date = position()
    parts = [(x_hbm.at[pl.ds((tile_rows - HB) * date, HB)], rows)]
    for p in range(n_par):
        column = pl.multiple_of(jnp.where(col % 2 == p, tile_cols - CW, 0), 8)
        parts.append((x_hbm.at[:, pl.ds(column, CW)], edges[p]))
    copies = [pltpu.make_async_copy(a, b, sems.at[k]) for k, (a, b) in enumerate(parts)]
    for copy in copies[::-1]:
        copy.start()
    for copy in copies:
        copy.wait()


def per_device(
    sizes, features, scene_shift, w_lat, b_lat, w_fpn, w_dec1, b_dec1, w_dec2, b_dec2, w_out, b_out
):
    _, n_rows, n_cols, _ = sizes
    tile_rows, tile_cols, chans = features.shape[1:]
    col, date = lax.axis_index("cols"), lax.axis_index("date")
    half, width = tile_rows // 2, tile_cols + 2 * CW
    n_par = 1 if n_cols == 2 else 2
    own = features[0]
    tile = pltpu.with_memory_space_constraint(own, pltpu.HBM)
    vmem = pl.BlockSpec(memory_space=pltpu.VMEM)
    kind = lambda *shape: jax.ShapeDtypeStruct(shape + (chans,), BF16)
    rows_own, *edges = pl.pallas_call(
        functools.partial(fetch_body, n_par, tile_rows, tile_cols),
        out_shape=(kind(HB, tile_cols),) + (kind(tile_rows, CW),) * n_par,
        in_specs=[pl.BlockSpec(memory_space=pltpu.HBM)],
        out_specs=(vmem,) * (1 + n_par),
        scratch_shapes=[pltpu.SemaphoreType.DMA((1 + n_par,))],
        compiler_params=pltpu.CompilerParams(vmem_limit_bytes=4 * 2**20),
        name="fetch",
    )(tile)
    first = date == 0

    def swap(value):
        return send(value, sizes, lambda r, c, d: (r, c, 1 - d))

    def edge(x, parity):
        return jnp.where(col % 2 == parity, x[:, tile_cols - CW :], x[:, :CW])

    def partner(c, parity):
        return column_partner(c, parity, n_cols)

    oth = swap(own)

    def shift_row(r, c, d):
        near = r - 1 + 2 * d
        return (near, c, 1 - d) if 0 <= near < n_rows else None

    def corner(p, r, c, d):
        near = shift_row(r, c, d)
        return None if near is None else (near[0], partner(c, p), near[2])

    mine, corners, others = [], [], []
    for p in range(n_par):
        mine.append(send(edges[p], sizes, lambda r, c, d, p=p: (r, partner(c, p), d)))
    rows_oth = lax.dynamic_slice_in_dim(oth, (tile_rows - HB) * date, HB, 0)
    for_row = jnp.concatenate(
        [
            jnp.where(first, rows_own[:HA], rows_oth[HB - HA :]),
            jnp.where(first, rows_oth, rows_own),
        ],
        axis=0,
    )
    from_row = send(for_row, sizes, shift_row)
    for p in range(n_par):
        others.append(swap(mine[p]))
    for p in range(n_par):
        corners.append(send(edge(for_row, p), sizes, functools.partial(corner, p)))
    shifts = [pltpu.SMEM(scene_shift.shape, jnp.int32), pltpu.SemaphoreType.DMA]
    lines_b = half + 4 + 2 * MO + 1

    def flat(lines, kind=F32):
        return jax.ShapeDtypeStruct((2 * CW + lines * width, chans), kind)

    def cat(lines, columns=width):
        return jax.ShapeDtypeStruct((lines, 3, columns, chans), BF16)

    def scratch(shape):
        return pltpu.VMEM(shape.shape, shape.dtype)

    def lines_of(lines):
        return jax.ShapeDtypeStruct((lines, width, chans), F32)

    pyr_a, pyr_b, *kept = pl.pallas_call(
        functools.partial(inner_body, n_par, n_cols, tile_rows, tile_cols),
        out_shape=(lines_of(half), flat(lines_b), cat(3), cat(3), cat(2), flat(2)),
        in_specs=[pl.BlockSpec(memory_space=pl.ANY)] + [vmem] * (2 + 2 * n_par + 5),
        out_specs=(vmem,) * 6,
        scratch_shapes=[
            scratch(flat(half + HA)),
            scratch(flat(half + HB)),
            scratch(cat(half + HA)),
            scratch(cat(half + HB)),
            scratch(cat(4)),
            scratch(flat(4)),
            *shifts,
        ],
        compiler_params=pltpu.CompilerParams(vmem_limit_bytes=28 * 2**20),
        cost_estimate=pl.CostEstimate(
            flops=2 * 10 * width * 1536 * 256, bytes_accessed=8 * 2**20, transcendentals=0
        ),
        name="inner",
    )(scene_shift, own, oth, *mine, *others, w_lat, b_lat[None], w_fpn, w_dec1, b_dec1[None])
    out, _ = pl.pallas_call(
        functools.partial(outer_body, n_par, n_rows, n_cols, tile_rows, tile_cols),
        out_shape=(jax.ShapeDtypeStruct((half, tile_cols), F32), flat(lines_b)),
        in_specs=[pl.BlockSpec(memory_space=pl.ANY)] + [vmem] * (n_par + 1 + 15),
        out_specs=(vmem,) * 2,
        input_output_aliases={n_par + 3: 1},
        scratch_shapes=[
            scratch(lines_of(4)),
            scratch(flat(HA + HB)),
            scratch(cat(HA)),
            scratch(cat(HB)),
            scratch(flat(half)),
            scratch(cat(half)),
            scratch(flat(half)),
            scratch(cat(half + 2, tile_cols)),
            *shifts,
        ],
        compiler_params=pltpu.CompilerParams(vmem_limit_bytes=24 * 2**20),
        name="outer",
    )(
        scene_shift, from_row, *corners, pyr_a, pyr_b, *kept,
        w_lat, b_lat[None], w_fpn, w_dec1, b_dec1[None], w_dec2, b_dec2[None], w_out[None],
        jnp.broadcast_to(b_out, (1, tile_cols)),
    )
    return out


def staged(sizes, *args):
    return per_device(sizes, *args)


def solution(mesh):
    sizes = tuple(mesh.shape[axis] for axis in ("groups", "rows", "cols", "date"))
    return jax.shard_map(
        functools.partial(staged, sizes),
        mesh=mesh,
        in_specs=(P("date", ("groups", "rows"), "cols", None), P("groups", None, None)) + (P(),) * 9,
        out_specs=P(("groups", "rows", "date"), "cols"),
        check_vma=False,
    )
```

```python
import functools

import jax
import jax.numpy as jnp
from jax import lax
from jax.experimental import pallas as pl
from jax.experimental.pallas import tpu as pltpu
from jax.sharding import PartitionSpec as P


MO = 4
HA = 3
HB = HA + MO
CW = 8
STRIP = 16
F32 = jnp.float32
BF16 = jnp.bfloat16


def column_partner(col, parity, n_cols):
    right = col % 2 == parity
    return (col + 1) % n_cols if right else (col - 1) % n_cols


def send(value, sizes, target):
    n_groups, n_rows, n_cols, n_dates = sizes

    def place(group, row, col, date):
        return ((group * n_rows + row) * n_cols + col) * n_dates + date

    pairs = []
    for group in range(n_groups):
        for row in range(n_rows):
            for col in range(n_cols):
                for date in range(n_dates):
                    to = target(row, col, date)
                    end = (
                        place((group + 1) % n_groups, row, col, date)
                        if to is None
                        else place(group, *to)
                    )
                    pairs.append((place(group, row, col, date), end))
    return lax.ppermute(value, ("groups", "rows", "cols", "date"), pairs)


def at(line, column, width):
    return CW + line * width + CW + column


def position():
    return lax.axis_index("rows"), lax.axis_index("cols"), lax.axis_index("date")


def put(target, line, column, width, value):
    start = at(line, column, width)
    target[start : start + value.shape[0]] = value


def gather(source, line, cat, index, count, column, width):
    start = at(line, column, width)
    for tap in range(3):
        cat[index, tap] = source[start + tap - 1 : start + tap - 1 + count].astype(BF16)


def conv(groups, w_ref, date, ways=2):
    taps = [w_ref[a + (2 - 2 * a) * date].reshape(-1, w_ref.shape[-1]) for a in range(3)]
    none = jnp.zeros_like(taps[0])
    tall = jnp.concatenate(
        [jnp.concatenate(taps + [none], axis=0), jnp.concatenate([none] + taps, axis=0)], axis=1
    )
    pairs = [lines[top : top + 4] for lines in groups for top in range(0, len(lines) - 2, 2)]
    outs = []
    for way in range(ways):
        some = pairs[way * len(pairs) // ways : (way + 1) * len(pairs) // ways]
        lines = [
            jnp.concatenate([pair[j][0][pair[j][1], tap] for pair in some], axis=0)
            for j in range(4)
            for tap in range(3)
        ]
        outs.append(jnp.dot(jnp.concatenate(lines, axis=1), tall, preferred_element_type=F32))
    return jnp.concatenate(outs, axis=0)


def run(cat, first, count):
    return [(cat, first + i) for i in range(count)]


def line_of(z, index, columns):
    chans = z.shape[1] // 2
    pair, k = divmod(index, 2)
    return z[pair * columns : (pair + 1) * columns, k * chans : (k + 1) * chans]


def put_sides(lat, line, col, n_cols, tile_cols, width, halves):
    even = col % 2 == 0
    right = halves[0] * (even & (col < n_cols - 1)).astype(F32)
    left = halves[0] * (~even).astype(F32)
    if len(halves) == 2:
        right = right + halves[1] * (~even & (col < n_cols - 1)).astype(F32)
        left = left + halves[1] * (even & (col > 0)).astype(F32)
    put(lat, line, -CW, width, left)
    put(lat, line, tile_cols, width, right)


def tile_columns(row, col, there, shift, date, n_cols, tile_cols, chans):
    cells = lax.broadcasted_iota(jnp.int32, (STRIP, chans), 0)
    tiles = []
    for step in (0, -1, 1):
        c = jnp.clip(col + step, 0, n_cols - 1)
        is_tile = (there & (col + step >= 0) & (col + step < n_cols)).astype(F32)
        sy, sx = shift[row, c, 0] * (1 - 2 * date), shift[row, c, 1]
        low = sx + step * tile_cols
        masks = []
        for left in (True, False):
            x = cells + (-CW if left else tile_cols + CW - STRIP)
            masks.append(((x >= low) & (x < low + tile_cols)).astype(F32) * is_tile)
        tiles.append((sy, sx, is_tile, masks[0], masks[1]))
    return tiles


def shares(count):
    share = jnp.where(count > 1.5, 0.5, 1.0)
    share = jnp.where(count > 2.5, 1.0 / 3.0, share)
    return jnp.where(count > 3.5, 0.25, share)


def difference(a_line, pyr_b, u, groups, inside, keep_line, width):
    plus = lambda x, y: y if x is None else x + y
    blank = pyr_b.shape[0] - CW - width
    count = [None, None]
    level = [None, None]
    middle, weight = None, 0.0
    for tiles, hit_of in groups:
        for k, (sy, sx, is_tile, *masks) in enumerate(tiles):
            start = CW + (u - sy + 2 + MO) * width - sx
            hit = None
            if hit_of is not None:
                hit = hit_of(sy).astype(F32)
                start = jnp.where(hit_of(sy), start, blank)
            for side in range(2):
                if k != 2 - side:
                    mask = masks[side] if hit is None else masks[side] * hit
                    count[side] = plus(count[side], mask)
                    strip = pyr_b[pl.ds(start + side * (width - STRIP), STRIP)] * masks[side]
                    level[side] = plus(level[side], strip)
            if k == 0:
                if hit is not None:
                    weight = weight + hit * is_tile
                    start = jnp.where(is_tile > 0, start, blank)
                middle = plus(middle, pyr_b[pl.ds(start + STRIP, width - 2 * STRIP)])
    outs = []
    for side in range(2):
        part = a_line[:STRIP] if side == 0 else a_line[width - STRIP :]
        value = jnp.abs(part - level[side] * shares(count[side]))
        keep = jnp.minimum(count[side], 1.0) * inside[side]
        outs.append(value * (keep if keep_line is None else keep * keep_line))
    part = a_line[STRIP : width - STRIP]
    if len(groups) == 1:
        middle = jnp.abs(part - middle)
    else:
        keep = jnp.minimum(weight, 1.0)
        keep = keep if keep_line is None else keep * keep_line
        middle = jnp.abs(part - middle * jnp.where(weight > 1.5, 0.5, 1.0)) * keep
    return jnp.concatenate([outs[0], middle, outs[1]], axis=0)


def grid_columns(col, n_cols, tile_cols, chans):
    x = lax.broadcasted_iota(jnp.int32, (STRIP, chans), 0) + col * tile_cols
    return [
        ((x + at >= 0) & (x + at < n_cols * tile_cols)).astype(F32)
        for at in (-CW, tile_cols + CW - STRIP)
    ]


def on_grid(line, inside, keep_line):
    parts = [line[:STRIP] * inside[0], line[STRIP:-STRIP], line[-STRIP:] * inside[1]]
    if keep_line is not None:
        parts = [part * keep_line for part in parts]
    return jnp.concatenate(parts, axis=0)


def inner_body(n_par, n_cols, tile_rows, tile_cols, shift_in, own, oth, *refs):
    mine, others = refs[:n_par], refs[n_par : 2 * n_par]
    (w_lat, b_lat, w_fpn, w_dec1, b_dec1,
     pyr_a, pyr_b, t_a, t_b, t_d, hid, lat_a, lat_b, cat_a, cat_b, cat_d, dif, shift, sem) = refs[2 * n_par :]
    shift_copy = pltpu.make_async_copy(shift_in, shift, sem)
    shift_copy.start()
    row, col, date = position()
    half, width, chans = tile_rows // 2, tile_cols + 2 * CW, own.shape[-1]
    weight, bias = w_lat[...], b_lat[...]

    def lateral(x):
        return jnp.dot(x, weight, preferred_element_type=F32) + bias

    for lat, cat, lines, is_own in (
        (lat_a, cat_a, half + HA, date == 0),
        (lat_b, cat_b, half + HB, date == 1),
    ):
        rows = [u + (tile_rows - 1 - 2 * u) * date for u in range(lines)]

        def pick(x, y, is_own=is_own):
            return jnp.where(is_own, x, y)

        z = lateral(jnp.concatenate([pick(own[t], oth[t]) for t in rows], axis=0))
        for u in range(lines):
            put(lat, u, 0, width, z[u * tile_cols : (u + 1) * tile_cols])
        z = [
            lateral(jnp.concatenate([pick(mine[p][t], others[p][t]) for t in rows], axis=0))
            for p in range(n_par)
        ]
        for u in range(lines):
            put_sides(lat, u, col, n_cols, tile_cols, width, [x[u * CW : (u + 1) * CW] for x in z])
        for u in range(lines):
            gather(lat, u, cat, u, width, -CW, width)
    for u in range(3):
        t_a[u] = cat_a[u]
        t_b[u] = cat_b[u]
    pairs_a, pairs_b = half // 2, half // 2 + MO // 2
    z = conv([run(cat_a, 1, 2 * pairs_a + 2), run(cat_b, 1, 2 * pairs_b + 2)], w_fpn, date)
    for i in range(2 * pairs_a):
        pyr_a[i] = line_of(z, i, width).astype(BF16).astype(F32)
    pyr_b[:CW] = jnp.zeros((CW, chans), F32)
    blank = pyr_b.shape[0] - CW - width
    pyr_b[blank:] = jnp.zeros((width + CW, chans), F32)
    for i in range(2 * pairs_b):
        line = line_of(z, 2 * pairs_a + i, width).astype(BF16).astype(F32)
        put(pyr_b, i + 4 + MO, -CW, width, line)

    shift_copy.wait()
    tiles = tile_columns(row, col, row >= 0, shift, date, n_cols, tile_cols, chans)
    inside = grid_columns(col, n_cols, tile_cols, chans)
    for i in range(4):
        u = i + half - 2
        value = difference(pyr_a[u - 2], pyr_b, u, [(tiles, None)], inside, None, width)
        put(dif, i, -CW, width, value)
    for i in range(4):
        gather(dif, i, cat_d, i, width, -CW, width)
    for i in range(2):
        t_d[i] = cat_d[i]
    z = conv([run(cat_d, 0, 4)], w_dec1, date, 1)
    z = jnp.maximum(z + jnp.concatenate([b_dec1[...]] * 2, 1), 0.0)
    for i in range(2):
        put(hid, i, -CW, width, on_grid(line_of(z, i, width), inside, None))


def outer_body(n_par, n_rows, n_cols, tile_rows, tile_cols, shift_in, v_ref, *refs):
    corners = refs[:n_par]
    (in_a, _, t_a, t_b, t_d, t_h, w_lat, b_lat, w_fpn, w_dec1, b_dec1, w_dec2, b_dec2, w_out, b_out,
     out_ref, pyr_b, pyr_a, lat, cat_a, cat_b, dif, cat_d, hid, cat_h, shift, sem) = refs[n_par:]
    shift_copy = pltpu.make_async_copy(shift_in, shift, sem)
    shift_copy.start()
    row, col, date = position()
    half, width, chans = tile_rows // 2, tile_cols + 2 * CW, w_lat.shape[-1]
    has_row = jnp.where(date == 0, row > 0, row < n_rows - 1)
    row_keep = has_row.astype(F32)
    weight, bias = jnp.where(has_row, w_lat[...], 0), b_lat[...] * row_keep

    def lateral(x):
        return jnp.dot(x, weight, preferred_element_type=F32) + bias

    lines = [i + (HA - 1 - 2 * i) * date for i in range(HA)]
    lines += [HA + i + (HB - 1 - 2 * i) * date for i in range(HB)]
    z = lateral(jnp.concatenate([v_ref[i] for i in lines], axis=0))
    for i in range(HA + HB):
        put(lat, i, 0, width, z[i * tile_cols : (i + 1) * tile_cols])
    z = [lateral(jnp.concatenate([corners[p][i] for i in lines], axis=0)) for p in range(n_par)]
    for i in range(HA + HB):
        put_sides(lat, i, col, n_cols, tile_cols, width, [x[i * CW : (i + 1) * CW] for x in z])
    for i in range(HA):
        gather(lat, i, cat_a, i, width, -CW, width)
    for i in range(HB):
        gather(lat, i + HA, cat_b, i, width, -CW, width)
    pairs_b = 2 + MO // 2
    z = conv([run(cat_a, 0, HA) + run(t_a, 0, 3), run(cat_b, 0, HB) + run(t_b, 0, 3)], w_fpn, date)
    for i in range(4):
        pyr_a[i] = line_of(z, i, width)
    for i in range(2 * pairs_b):
        put(pyr_b, i, -CW, width, line_of(z, 4 + i, width))

    near_row = jnp.clip(row + jnp.where(date == 0, -1, 1), 0, n_rows - 1)
    shift_copy.wait()
    tiles = tile_columns(row, col, row >= 0, shift, date, n_cols, tile_cols, chans)
    near = tile_columns(near_row, col, has_row, shift, date, n_cols, tile_cols, chans)
    inside = grid_columns(col, n_cols, tile_cols, chans)
    for i in range(half):
        u = i - 2
        groups = [(tiles, None)]
        if u < MO:
            groups = [
                (tiles, lambda sy, u=u: u - sy >= 0),
                (near, lambda sy, u=u: u - sy < 0),
            ]
        a_line = pyr_a[u + 2] if u < 2 else in_a[u - 2]
        value = difference(a_line, pyr_b, u, groups, inside, row_keep if u < 0 else None, width)
        put(dif, i, -CW, width, value)
    for i in range(half):
        gather(dif, i, cat_d, i, width, -CW, width)
    z = conv([run(cat_d, 0, half) + run(t_d, 0, 2)], w_dec1, date)
    z = jnp.maximum(z + jnp.concatenate([b_dec1[...]] * 2, 1), 0.0)
    for i in range(half):
        put(hid, i, -CW, width, on_grid(line_of(z, i, width), inside, None if i else row_keep))
    for i in range(half):
        gather(hid, i, cat_h, i, tile_cols, 0, width)
    for i in range(2):
        gather(t_h, i, cat_h, i + half, tile_cols, 0, width)
    z = conv([run(cat_h, 0, half + 2)], w_dec2, date)
    z = jnp.maximum(z + jnp.concatenate([b_dec2[...]] * 2, 1), 0.0).astype(BF16)
    none = jnp.zeros((1, chans), BF16)
    upper = jnp.concatenate([w_out[...], none], axis=1)
    lower = jnp.concatenate([none, w_out[...]], axis=1)
    weight = jnp.concatenate([upper, lower] * 8, axis=0)
    logit = lax.dot_general(weight, z, (((1,), (1,)), ((), ())), preferred_element_type=F32)
    for i in range(half):
        pair, k = divmod(i, 2)
        line = logit[k : k + 1, pair * tile_cols : (pair + 1) * tile_cols] + b_out[...]
        out_ref[pl.ds(i + (half - 1 - 2 * i) * date, 1)] = line


def fetch_body(n_par, tile_rows, tile_cols, x_hbm, rows, *refs):
    edges, sems = refs[:n_par], refs[n_par]
    _, col, date = position()
    parts = [(x_hbm.at[pl.ds((tile_rows - HB) * date, HB)], rows)]
    for p in range(n_par):
        column = pl.multiple_of(jnp.where(col % 2 == p, tile_cols - CW, 0), 8)
        parts.append((x_hbm.at[:, pl.ds(column, CW)], edges[p]))
    copies = [pltpu.make_async_copy(a, b, sems.at[k]) for k, (a, b) in enumerate(parts)]
    for copy in copies[::-1]:
        copy.start()
    for copy in copies:
        copy.wait()


def per_device(
    sizes, features, scene_shift, w_lat, b_lat, w_fpn, w_dec1, b_dec1, w_dec2, b_dec2, w_out, b_out
):
    _, n_rows, n_cols, _ = sizes
    tile_rows, tile_cols, chans = features.shape[1:]
    col, date = lax.axis_index("cols"), lax.axis_index("date")
    half, width = tile_rows // 2, tile_cols + 2 * CW
    n_par = 1 if n_cols == 2 else 2
    own = features[0]
    tile = pltpu.with_memory_space_constraint(own, pltpu.HBM)
    vmem = pl.BlockSpec(memory_space=pltpu.VMEM)
    kind = lambda *shape: jax.ShapeDtypeStruct(shape + (chans,), BF16)
    rows_own, *edges = pl.pallas_call(
        functools.partial(fetch_body, n_par, tile_rows, tile_cols),
        out_shape=(kind(HB, tile_cols),) + (kind(tile_rows, CW),) * n_par,
        in_specs=[pl.BlockSpec(memory_space=pltpu.HBM)],
        out_specs=(vmem,) * (1 + n_par),
        scratch_shapes=[pltpu.SemaphoreType.DMA((1 + n_par,))],
        compiler_params=pltpu.CompilerParams(vmem_limit_bytes=4 * 2**20),
        name="fetch",
    )(tile)
    first = date == 0

    def swap(value):
        return send(value, sizes, lambda r, c, d: (r, c, 1 - d))

    def edge(x, parity):
        return jnp.where(col % 2 == parity, x[:, tile_cols - CW :], x[:, :CW])

    def partner(c, parity):
        return column_partner(c, parity, n_cols)

    oth = swap(own)

    def shift_row(r, c, d):
        near = r - 1 + 2 * d
        return (near, c, 1 - d) if 0 <= near < n_rows else None

    def corner(p, r, c, d):
        near = shift_row(r, c, d)
        return None if near is None else (near[0], partner(c, p), near[2])

    mine, corners, others = [], [], []
    for p in range(n_par):
        mine.append(send(edges[p], sizes, lambda r, c, d, p=p: (r, partner(c, p), d)))
    rows_oth = lax.dynamic_slice_in_dim(oth, (tile_rows - HB) * date, HB, 0)
    for_row = jnp.concatenate(
        [
            jnp.where(first, rows_own[:HA], rows_oth[HB - HA :]),
            jnp.where(first, rows_oth, rows_own),
        ],
        axis=0,
    )
    from_row = send(for_row, sizes, shift_row)
    for p in range(n_par):
        others.append(swap(mine[p]))
    for p in range(n_par):
        corners.append(send(edge(for_row, p), sizes, functools.partial(corner, p)))
    shifts = [pltpu.SMEM(scene_shift.shape, jnp.int32), pltpu.SemaphoreType.DMA]
    lines_b = half + 4 + 2 * MO + 1

    def flat(lines, kind=F32):
        return jax.ShapeDtypeStruct((2 * CW + lines * width, chans), kind)

    def cat(lines, columns=width):
        return jax.ShapeDtypeStruct((lines, 3, columns, chans), BF16)

    def scratch(shape):
        return pltpu.VMEM(shape.shape, shape.dtype)

    def lines_of(lines):
        return jax.ShapeDtypeStruct((lines, width, chans), F32)

    pyr_a, pyr_b, *kept = pl.pallas_call(
        functools.partial(inner_body, n_par, n_cols, tile_rows, tile_cols),
        out_shape=(lines_of(half), flat(lines_b), cat(3), cat(3), cat(2), flat(2)),
        in_specs=[pl.BlockSpec(memory_space=pl.ANY)] + [vmem] * (2 + 2 * n_par + 5),
        out_specs=(vmem,) * 6,
        scratch_shapes=[
            scratch(flat(half + HA)),
            scratch(flat(half + HB)),
            scratch(cat(half + HA)),
            scratch(cat(half + HB)),
            scratch(cat(4)),
            scratch(flat(4)),
            *shifts,
        ],
        compiler_params=pltpu.CompilerParams(vmem_limit_bytes=28 * 2**20),
        cost_estimate=pl.CostEstimate(
            flops=2 * 10 * width * 1536 * 256, bytes_accessed=8 * 2**20, transcendentals=0
        ),
        name="inner",
    )(scene_shift, own, oth, *mine, *others, w_lat, b_lat[None], w_fpn, w_dec1, b_dec1[None])
    out, _ = pl.pallas_call(
        functools.partial(outer_body, n_par, n_rows, n_cols, tile_rows, tile_cols),
        out_shape=(jax.ShapeDtypeStruct((half, tile_cols), F32), flat(lines_b)),
        in_specs=[pl.BlockSpec(memory_space=pl.ANY)] + [vmem] * (n_par + 1 + 15),
        out_specs=(vmem,) * 2,
        input_output_aliases={n_par + 3: 1},
        scratch_shapes=[
            scratch(lines_of(4)),
            scratch(flat(HA + HB)),
            scratch(cat(HA)),
            scratch(cat(HB)),
            scratch(flat(half)),
            scratch(cat(half)),
            scratch(flat(half)),
            scratch(cat(half + 2, tile_cols)),
            *shifts,
        ],
        compiler_params=pltpu.CompilerParams(vmem_limit_bytes=24 * 2**20),
        name="outer",
    )(
        scene_shift, from_row, *corners, pyr_a, pyr_b, *kept,
        w_lat, b_lat[None], w_fpn, w_dec1, b_dec1[None], w_dec2, b_dec2[None], w_out[None],
        jnp.broadcast_to(b_out, (1, tile_cols)),
    )
    return out


def staged(sizes, *args):
    return per_device(sizes, *args)


def solution(mesh):
    sizes = tuple(mesh.shape[axis] for axis in ("groups", "rows", "cols", "date"))
    return jax.shard_map(
        functools.partial(staged, sizes),
        mesh=mesh,
        in_specs=(P("date", ("groups", "rows"), "cols", None), P("groups", None, None)) + (P(),) * 9,
        out_specs=P(("groups", "rows", "date"), "cols"),
        check_vma=False,
    )
```
